32 devices in a mesh: phase: 2 (over core), tok: 4 (over z), mp: 4 (over y, x).
Axes of the slice: x: 2, y: 2, z: 4, core: 2. Of those that a mesh axis runs over, the one named last changes fastest.
Arguments:
- hidden: bfloat16 [2, 512, 6656], P('phase', 'tok', 'mp'), may hold values from -30 to 30
- w_qkv: bfloat16 [2, 6656, 3, 4096], P('phase', 'mp', None, 'tok'), may hold values from -1 to 1
- segment_ids: int32 [2, 512], P('phase'), may hold values from 0 to 3, never falling along the last dimension, each value on 1 to 256 neighbouring positions
- exit_flags: int32 [2, 4], P('phase'), may hold values from 0 to 1, as said below
Outputs:
- attended: bfloat16 [2, 512, 4096], P('phase', 'mp', 'tok')
- handed: bfloat16 [2, 512, 4096], P('phase', 'mp', 'tok')
The draws below stay inside these ranges and needn't reach their ends.
Inputs may be any that keep to these rules, and one draw needn't show every extreme that they name: `exit_flags`: in each micro-batch exactly 2 of the 4 blocks have flag 0.
All inputs are finite; a program needn't handle non-finite values.
Results may differ from the reference program's by a relative error of at most 0.0068.
Values may be sent and summed in bfloat16 or wider, within the bound.
A program may use at most 64 MiB of HBM per device.

```python
import math
import jax
import jax.numpy as jnp
import numpy as np
from jax import lax

D = 6656
HEADS = 32
HEAD = 128
BLOCK = 128
SEGS = 4
TOKENS = 512
BLOCKS = 4
SURV_BLK = 2
N_PHASE = 2


def draw_hidden(key, part):
    first = jax.random.fold_in(key, 11)
    rows = jnp.clip(jax.random.normal(first, (N_PHASE, TOKENS, D), jnp.float32), -6.0, 6.0)
    return rows.astype(jnp.bfloat16)


def draw_w_qkv(key, part):
    first = jax.random.fold_in(key, 21)
    weights = jnp.clip(jax.random.normal(first, (N_PHASE, D, 3, HEADS * HEAD), jnp.float32), -4.0, 4.0) / math.sqrt(D)
    return weights.astype(jnp.bfloat16)


def draw_exit_flags(key, part):
    first = jax.random.fold_in(key, 31)
    phase_keys = jax.random.split(first, N_PHASE)
    ranks = jax.vmap(lambda one: jax.random.permutation(one, BLOCKS))(phase_keys)
    return (ranks >= SURV_BLK).astype(jnp.int32)


def length_profile(count, total, bound, lean):
    portions = [(1 << 20) // math.isqrt(grade ** lean) + 1 for grade in range(2, count + 1)]
    rest, counts = total - bound - (count - 1), [1] * (count - 1)
    while rest > 0:
        candidates = [i for i in range(count - 1) if counts[i] < bound]
        mass, remaining = sum([portions[i] for i in candidates]), rest
        for i in candidates:
            more = min(bound - counts[i], max(1, remaining * portions[i] // mass), rest)
            counts[i] = counts[i] + more
            rest = rest - more
    return np.array([bound] + counts)


def ragged_sizes(key, number_of, total, most, skew):
    if number_of == 2:
        one = jax.random.randint(key, (), max(1, total - most), min(most, total - 1) + 1)
        return jnp.stack([one, total - one])
    tallies = jnp.asarray(length_profile(number_of, total, most, skew), jnp.int32)
    pairs = (number_of - 1) // 2
    giver, taker = tallies[1:1 + 2 * pairs:2], tallies[2:2 + 2 * pairs:2]
    slack = jnp.minimum(giver - 1, most - taker)
    passed = jax.random.randint(jax.random.fold_in(key, 1), (pairs,), 0, 1 << 20) % (slack + 1)
    tallies = tallies.at[1:1 + 2 * pairs:2].set(giver - passed).at[2:2 + 2 * pairs:2].set(taker + passed)
    return tallies[jax.random.permutation(jax.random.fold_in(key, 2), number_of)]


def setup_inputs(seed: int = 0) -> dict:
    key_of = jax.random.split(jax.random.key(seed), 5)
    hidden = draw_hidden(jax.random.fold_in(key_of[4], 71), 0)
    w_qkv = draw_w_qkv(jax.random.fold_in(key_of[4], 71), 0)
    segment_ids = jax.vmap(lambda own: jnp.searchsorted(jnp.cumsum(ragged_sizes(own, SEGS, TOKENS, TOKENS // 2, 0)), jnp.arange(TOKENS), side="right"))(jax.random.split(key_of[2], N_PHASE)).reshape((N_PHASE, TOKENS)).astype(jnp.int32)
    exit_flags = draw_exit_flags(jax.random.fold_in(key_of[4], 71), 0)
    return dict(hidden=hidden, w_qkv=w_qkv, segment_ids=segment_ids, exit_flags=exit_flags)


def attend_head(trio, segment):
    query, keys, values = trio
    total = query.shape[0]
    scores = jnp.dot(query, keys.T, preferred_element_type=jnp.float32) * (1.0 / math.sqrt(HEAD))
    positions = jnp.arange(total, dtype=jnp.int32)
    allowed = (positions[None, :] <= positions[:, None]) & (segment[None, :] == segment[:, None])
    scores = jnp.where(allowed, scores, -1e+30)
    peak = lax.optimization_barrier(jnp.max(scores, axis=-1, keepdims=True))
    expo = jnp.exp(scores - peak)
    probs = (expo / lax.optimization_barrier(jnp.sum(expo, axis=-1, keepdims=True))).astype(jnp.bfloat16)
    return jnp.dot(probs, values, preferred_element_type=jnp.float32)

def reference(hidden, w_qkv, segment_ids, exit_flags):
    results = []
    for phase in range(N_PHASE):
        rows = hidden[phase]
        query = jnp.dot(rows, w_qkv[phase, :, 0, :], preferred_element_type=jnp.float32).astype(jnp.bfloat16)
        keys = jnp.dot(rows, w_qkv[phase, :, 1, :], preferred_element_type=jnp.float32).astype(jnp.bfloat16)
        values = jnp.dot(rows, w_qkv[phase, :, 2, :], preferred_element_type=jnp.float32).astype(jnp.bfloat16)

        def split_heads(matrix):
            return matrix.reshape(TOKENS, HEADS, HEAD).transpose(1, 0, 2)
        segment = segment_ids[phase]
        mixed = lax.map(lambda trio: attend_head(trio, segment), (split_heads(query), split_heads(keys), split_heads(values)))
        mixed = mixed.transpose(1, 0, 2).reshape(TOKENS, HEADS * HEAD)
        alive = jnp.repeat(exit_flags[phase] == 0, BLOCK)
        results.append(jnp.where(alive[:, None], mixed, 0.0).astype(jnp.bfloat16))
    attended = jnp.stack(results)
    handed = jnp.roll(attended, 1, axis=0)
    return (attended, handed)
```

```python
import math

import jax
import jax.numpy as jnp
from jax import lax
from jax.experimental import pallas as pl
from jax.experimental.pallas import tpu as pltpu
from jax.sharding import PartitionSpec as P

HEAD = 128
BLOCK = 128
CHUNKS = 2
TIERS = 4
GROUPS = 4
MESH = pl.DeviceIdType.MESH


def remote(src, dst, send, recv, where):
    return pltpu.make_async_remote_copy(
        src_ref=src, dst_ref=dst, send_sem=send, recv_sem=recv, device_id=where, device_id_type=MESH
    )


def fused_kernel(
    x_hbm, w_ref, seg_hbm, flag_hbm, att_ref, hand_ref,
    hid, wbuf, seg_ref, flag_ref, send1, recv1, send2, recv2, keep, acc, qkv, outb,
    own_sem, small_sem, w_sem, up_sem, down_sem, gather_sem,
    s1_send, s1_recv, s2_send, s2_recv, a_send, a_recv, h_send, h_recv,
):
    p = lax.axis_index("phase")
    z = lax.axis_index("tok")
    m = lax.axis_index("mp")
    tiers = TIERS
    groups = GROUPS
    rows = x_hbm.shape[0]
    piece = rows // CHUNKS
    cols = w_ref.shape[2] // groups
    half = cols // 2
    part3 = 3 * half
    total = rows * tiers
    quarter = total // groups
    scale = 1.0 / math.sqrt(HEAD)
    peer = [m, m + 1 - 2 * (m % 2), (m + 2) % groups, groups - 1 - m]
    ends = (z == 0) | (z == tiers - 1)
    low = z < tiers // 2

    def columns(member):
        return pl.ds(pl.multiple_of(member * cols, HEAD), cols)

    own = pltpu.make_async_copy(x_hbm, hid.at[z], own_sem)
    own.start()

    def weights(j):
        return pltpu.make_async_copy(w_ref.at[:, :, columns(peer[j])], wbuf.at[j], w_sem.at[j])

    for j in (3, 1, 2, 0):
        weights(j).start()
    segments = pltpu.make_async_copy(seg_hbm, seg_ref, small_sem.at[0])
    segments.start()
    flags = pltpu.make_async_copy(flag_hbm, flag_ref, small_sem.at[1])
    flags.start()

    barrier = pltpu.get_barrier_semaphore()

    @pl.when(z > 0)
    def _():
        pl.semaphore_signal(barrier, inc=1, device_id={"tok": z - 1}, device_id_type=MESH)

    @pl.when(z < tiers - 1)
    def _():
        pl.semaphore_signal(barrier, inc=1, device_id={"tok": z + 1}, device_id_type=MESH)

    for j in (1, 2):
        pl.semaphore_signal(barrier, inc=1, device_id={"mp": peer[j]}, device_id_type=MESH)
    pl.semaphore_signal(barrier, inc=1, device_id={"phase": 1 - p}, device_id_type=MESH)

    def part(c):
        return pl.ds(pl.multiple_of(c * piece, piece), piece)

    def upward(t, c):
        ref = hid.at[t, part(c)]
        return remote(ref, ref, up_sem.at[t, c], gather_sem.at[t, c], {"tok": z + 1})

    def downward(t, c):
        ref = hid.at[t, part(c)]
        return remote(ref, ref, down_sem.at[t, c], gather_sem.at[t, c], {"tok": z - 1})

    def first(j, t, c):
        return remote(
            send1.at[j - 1, t, part(c)], recv1.at[j - 1, t, part(c)],
            s1_send.at[j - 1, t, c], s1_recv.at[j - 1, t, c], {"mp": peer[j]},
        )

    def second(j, t, c):
        return remote(
            send2.at[j - 1, t, part(c)], recv2.at[j - 1, t, part(c)],
            s2_send.at[j - 1, t, c], s2_recv.at[j - 1, t, c], {"mp": peer[j]},
        )

    def place(n):
        s, c = n // CHUNKS, n % CHUNKS
        end_t = jnp.where(low, z + s, z - s)
        near = jnp.where(low, z, tiers - 1 - z)
        inner_t = jnp.where(c == 0, z - 1, z + 1)
        inner_c = s - 1
        far_t = jnp.where(low, z + 2, z - 2)
        t = jnp.where(ends, end_t, jnp.where(s == 0, z, jnp.where(s == tiers - 1, far_t, inner_t)))
        c = jnp.where(ends | (s == 0) | (s == tiers - 1), c, inner_c)
        return t, c

    def product(j, k, t, span):
        return jnp.dot(hid[t, span, :], wbuf[j, k], preferred_element_type=jnp.float32)

    def multiply(j, t, span):
        for k in range(3):
            at = slice(k * half, (k + 1) * half)
            later = slice(part3 + k * half, part3 + (k + 1) * half)
            got = product(j, k, t, span)
            if j == 0:
                acc[0, t, span, at] = got[:, :half]
                acc[1, t, span, at] = got[:, half:]
                continue
            if j == 3:
                send1[0, t, span, later] = got[:, :half].astype(jnp.bfloat16)
                send1[1, t, span, later] = got[:, half:].astype(jnp.bfloat16)
            elif j == 1:
                send1[0, t, span, at] = got[:, :half].astype(jnp.bfloat16)
                keep[0, t, span, at] = got[:, half:]
            else:
                send1[1, t, span, at] = got[:, half:].astype(jnp.bfloat16)
                keep[1, t, span, at] = got[:, :half]

    def combine(n):
        t, c = place(n)
        span = part(c)
        for j in (1, 2):
            first(j, t, c).wait_recv()
        for j in (1, 2):
            got = recv1[2 - j, t, span, part3:].astype(jnp.float32)
            send2[j - 1, t, span, :] = (keep[j - 1, t, span, :] + got).astype(jnp.bfloat16)
            second(j, t, c).start()

    def finish(n):
        t, c = place(n)
        span = part(c)
        for j in (1, 2):
            second(j, t, c).wait_recv()
        start = pl.multiple_of(t * rows + c * piece, piece)
        for h in range(2):
            value = (
                acc[h, t, span, :]
                + recv1[h, t, span, :part3].astype(jnp.float32)
                + recv2[1 - h, t, span, :].astype(jnp.float32)
            ).astype(jnp.bfloat16)
            for k in range(3):
                qkv[k, pl.ds(start, piece), h * half : (h + 1) * half] = value[
                    :, k * half : (k + 1) * half
                ]

    def arrive(n, onward):
        t, c = place(n)

        @pl.when(t < z)
        def _():
            upward(t, c).wait_recv()
            if onward:
                upward(t, c).start()

        @pl.when(t > z)
        def _():
            downward(t, c).wait_recv()
            if onward:
                downward(t, c).start()

    own.wait()
    everything = pl.ds(0, rows)
    for j in (3, 1, 2, 0):
        weights(j).wait()
        multiply(j, z, everything)

    pl.semaphore_wait(barrier, 3 + jnp.minimum(z, 1) + jnp.minimum(tiers - 1 - z, 1))

    for c in range(CHUNKS):

        @pl.when(z < tiers - 1)
        def _():
            upward(z, c).start()

        @pl.when(z > 0)
        def _():
            downward(z, c).start()

    for c in range(CHUNKS):
        for j in (1, 2):
            first(j, z, c).start()

    ahead = jnp.where(ends, 1, 0)

    @pl.when(ends)
    def _():
        combine(0)

    @pl.loop(CHUNKS, tiers * CHUNKS)
    def _(n):
        k = n - 2 + ahead
        combine(k)

        @pl.when(k > 0)
        def _():
            finish(k - 1)

        @pl.when(ends)
        def _():
            arrive(n, False)

        @pl.when(jnp.logical_not(ends) & (n % CHUNKS == 0) & (n < (tiers - 1) * CHUNKS))
        def _():
            arrive(n, True)
            arrive(n + 1, True)

        @pl.when(jnp.logical_not(ends) & (n >= (tiers - 1) * CHUNKS))
        def _():
            arrive(n, True)

        t, c = place(n)
        span = part(c)
        multiply(3, t, span)
        for j in (1, 2):
            multiply(j, t, span)
            first(j, t, c).start()
        multiply(0, t, span)

    last = tiers * CHUNKS - 1

    @pl.when(jnp.logical_not(ends))
    def _():
        combine(last - 1)
        finish(last - 2)

    combine(last)
    finish(last - 1)
    finish(last)

    segments.wait()
    flags.wait()

    def exchange(j):
        return remote(
            outb.at[j - 1], att_ref.at[:, columns(m)], a_send.at[j - 1], a_recv.at[j - 1],
            {"mp": (m + j) % groups},
        )

    def hand(j, member, src):
        return remote(
            src, hand_ref.at[:, columns(member)], h_send.at[j - 1], h_recv.at[j - 1],
            {"phase": 1 - p},
        )

    seg_keys = seg_ref[...]
    key_pos = lax.broadcasted_iota(jnp.int32, (BLOCK, total), 1)
    row_pos = lax.broadcasted_iota(jnp.int32, (BLOCK, total), 0)

    @pl.loop(1, groups + 1)
    def _(j):
        r = (m + j) % groups
        for b in range(quarter // BLOCK):
            first = pl.multiple_of(r * quarter + b * BLOCK, BLOCK)
            here = pl.ds(first, BLOCK)
            seg_rows = jnp.broadcast_to(seg_ref[:, here], (BLOCK, BLOCK)).T
            seg_rows = jnp.concatenate([seg_rows] * (total // BLOCK), axis=1)
            allowed = (key_pos <= row_pos + first) & (seg_rows == seg_keys)
            flag = flag_ref[0, r * (quarter // BLOCK) + b]
            kept = jnp.full((BLOCK, HEAD), flag, jnp.int32) == 0
            for h in range(cols // HEAD):
                head = slice(h * HEAD, (h + 1) * HEAD)
                scores = (
                    lax.dot_general(
                        qkv[0, here, head], qkv[1, :, head], (((1,), (1,)), ((), ())),
                        preferred_element_type=jnp.float32,
                    )
                    * scale
                )
                scores = jnp.where(allowed, scores, -1e30)
                peak = jnp.max(scores, axis=-1, keepdims=True)
                expo = jnp.exp(scores - peak)
                probs = (expo / jnp.sum(expo, axis=-1, keepdims=True)).astype(jnp.bfloat16)
                mixed = jnp.dot(probs, qkv[2, :, head], preferred_element_type=jnp.float32)
                outb[j - 1, b * BLOCK : (b + 1) * BLOCK, head] = jnp.where(
                    kept, mixed, 0.0
                ).astype(jnp.bfloat16)

        @pl.when(j < groups)
        def _():
            exchange(j).start()

    hand(groups, m, outb.at[groups - 1]).start()
    att_ref[:, columns(m)] = outb[groups - 1]
    for j in range(1, groups):
        member = (m + groups - j) % groups
        exchange(j).wait_recv()
        hand(j, member, att_ref.at[:, columns(member)]).start()

    for c in range(CHUNKS):
        for t in range(tiers):

            @pl.when((z >= t) & (z < tiers - 1))
            def _():
                upward(t, c).wait_send()

            @pl.when((z <= t) & (z > 0))
            def _():
                downward(t, c).wait_send()

            for j in (1, 2):
                first(j, t, c).wait_send()
                second(j, t, c).wait_send()

    for j in range(1, groups):
        exchange(j).wait_send()
    for j in range(1, groups + 1):
        hand(j, m, outb.at[groups - 1]).wait()


def local_fused(hidden, w_qkv, segment_ids, exit_flags):
    rows = hidden[0]
    weights = jnp.transpose(w_qkv[0], (1, 0, 2))
    tiers = lax.axis_size("tok")
    groups = lax.axis_size("mp")
    count, width = rows.shape
    head_cols = weights.shape[2]
    cols = head_cols // groups
    total = count * tiers
    quarter = total // groups
    half = cols // 2
    out = jax.ShapeDtypeStruct((quarter, head_cols), jnp.bfloat16)
    dma = pltpu.SemaphoreType.DMA
    pieces = (2, tiers, CHUNKS)
    attended, handed = pl.pallas_call(
        fused_kernel,
        out_shape=(out, out),
        in_specs=[pl.BlockSpec(memory_space=pl.ANY)] * 4,
        out_specs=(pl.BlockSpec(memory_space=pltpu.VMEM),) * 2,
        scratch_shapes=[
            pltpu.VMEM((tiers, count, width), jnp.bfloat16),
            pltpu.VMEM((groups, 3, width, cols), jnp.bfloat16),
            pltpu.VMEM(segment_ids.shape, jnp.int32),
            pltpu.SMEM(exit_flags.shape, jnp.int32),
            pltpu.VMEM((2, tiers, count, 6 * half), jnp.bfloat16),
            pltpu.VMEM((2, tiers, count, 6 * half), jnp.bfloat16),
            pltpu.VMEM((2, tiers, count, 3 * half), jnp.bfloat16),
            pltpu.VMEM((2, tiers, count, 3 * half), jnp.bfloat16),
            pltpu.VMEM((2, tiers, count, 3 * half), jnp.float32),
            pltpu.VMEM((2, tiers, count, 3 * half), jnp.float32),
            pltpu.VMEM((3, total, cols), jnp.bfloat16),
            pltpu.VMEM((groups, quarter, cols), jnp.bfloat16),
            dma(()),
            dma((2,)),
            dma((groups,)),
            dma((tiers, CHUNKS)),
            dma((tiers, CHUNKS)),
            dma((tiers, CHUNKS)),
            dma(pieces),
            dma(pieces),
            dma(pieces),
            dma(pieces),
            dma((groups - 1,)),
            dma((groups - 1,)),
            dma((groups,)),
            dma((groups,)),
        ],
        compiler_params=pltpu.CompilerParams(
            collective_id=0, has_side_effects=True, vmem_limit_bytes=60 * 1024 * 1024
        ),
    )(rows, weights, segment_ids, exit_flags)
    return (attended[None], handed[None])


def shifted(block, axis, distance):
    devices = range(lax.axis_size(axis))
    route = [((i - distance) % len(devices), i) for i in devices]
    return lax.ppermute(block, axis, route)


def attend(query, keys, values, query_pos, segment, key_pos):
    heads_here = query.shape[1] // HEAD
    total = keys.shape[0]
    key_heads = keys.reshape(total, heads_here, HEAD)
    value_heads = values.reshape(total, heads_here, HEAD)
    key_segment = jnp.take(segment, key_pos)
    scale = 1.0 / math.sqrt(HEAD)
    block_rows = query.shape[0]
    scores = (
        jnp.einsum(
            "rhd,shd->hrs",
            query.reshape(block_rows, heads_here, HEAD),
            key_heads,
            preferred_element_type=jnp.float32,
        )
        * scale
    )
    own_segment = jnp.take(segment, query_pos)
    allowed = (key_pos[None, :] <= query_pos[:, None]) & (
        key_segment[None, :] == own_segment[:, None]
    )
    scores = jnp.where(allowed[None], scores, -1e30)
    peak = jnp.max(scores, axis=-1, keepdims=True)
    expo = jnp.exp(scores - peak)
    probs = (expo / jnp.sum(expo, axis=-1, keepdims=True)).astype(jnp.bfloat16)
    mixed = jnp.einsum("hrs,shd->rhd", probs, value_heads, preferred_element_type=jnp.float32)
    return mixed.reshape(block_rows, heads_here * HEAD).astype(jnp.bfloat16)


def local(hidden, w_qkv, segment_ids, exit_flags):
    rows_here = hidden[0]
    weights = w_qkv[0]
    width_here = rows_here.shape[1]
    head_cols = weights.shape[2]
    flat_weights = weights.reshape(width_here, 3 * head_cols)
    segment = segment_ids[0]
    flags = exit_flags[0]
    groups = lax.axis_size("mp")
    member = lax.axis_index("mp")
    partial_value = jnp.dot(
        lax.all_gather(rows_here, "tok", axis=0, tiled=True),
        flat_weights,
        preferred_element_type=jnp.float32,
    )
    total = partial_value.shape[0]
    quarter = total // groups
    query_part = partial_value[:, :head_cols]
    key_value_part = partial_value[:, head_cols:]
    my_pos = member * quarter + jnp.arange(quarter, dtype=jnp.int32)
    my_blocks = my_pos // BLOCK
    alive = jnp.take(flags, my_blocks) == 0
    query = lax.psum_scatter(query_part, "mp", scatter_dimension=0, tiled=True).astype(jnp.bfloat16)
    mine = lax.psum_scatter(key_value_part, "mp", scatter_dimension=0, tiled=True).astype(
        jnp.bfloat16
    )
    key_value = lax.all_gather(mine, "mp", axis=0, tiled=True)
    all_pos = jnp.arange(total, dtype=jnp.int32)
    mixed = attend(
        query, key_value[:, :head_cols], key_value[:, head_cols:], my_pos, segment, all_pos
    )
    zeros = jnp.zeros((quarter, head_cols), jnp.bfloat16)
    result = jnp.where(alive[:, None], mixed, zeros)
    handed = shifted(result, "phase", 1)
    return (result[None], handed[None])


def solution(mesh):
    in_specs = (
        P("phase", "tok", "mp"),
        P("phase", "mp", None, "tok"),
        P("phase", None),
        P("phase", None),
    )
    out_specs = (P("phase", "mp", "tok"), P("phase", "mp", "tok"))
    sizes = dict(mesh.shape)

    def step(hidden, w_qkv, segment_ids, exit_flags):
        heads_here = w_qkv.shape[3] // sizes["tok"] // HEAD
        quarter = hidden.shape[1] // sizes["mp"]
        by_head = (
            heads_here % (2 * sizes["mp"]) == 0
            and quarter % BLOCK == 0
            and (sizes["phase"], sizes["tok"], sizes["mp"]) == (2, TIERS, GROUPS)
        )
        body = local_fused if by_head else local
        return jax.shard_map(
            body, mesh=mesh, in_specs=in_specs, out_specs=out_specs, check_vma=False
        )(hidden, w_qkv, segment_ids, exit_flags)

    return step
```

```python
import math

import jax
import jax.numpy as jnp
from jax import lax
from jax.experimental import pallas as pl
from jax.experimental.pallas import tpu as pltpu
from jax.sharding import PartitionSpec as P

HEAD = 128
BLOCK = 128
TIERS = 4
GROUPS = 4
MESH = pl.DeviceIdType.MESH


def remote(src, dst, send, recv, where):
    return pltpu.make_async_remote_copy(
        src_ref=src, dst_ref=dst, send_sem=send, recv_sem=recv, device_id=where, device_id_type=MESH
    )


def fused_kernel(
    x_hbm, w_ref, seg_hbm, flag_hbm, att_ref, hand_ref,
    hid, wbuf, seg_ref, flag_ref, send1, recv1, send2, recv2, keep, acc, qkv, outb,
    own_sem, small_sem, w_sem, up_sem, down_sem, gather_sem,
    s1_send, s1_recv, s2_send, s2_recv, a_send, a_recv, h_send, h_recv,
):
    p = lax.axis_index("phase")
    z = lax.axis_index("tok")
    m = lax.axis_index("mp")
    tiers = TIERS
    groups = GROUPS
    rows = x_hbm.shape[0]
    cols = w_ref.shape[2] // groups
    half = cols // 2
    part3 = 3 * half
    total = rows * tiers
    piece = rows // 2
    small = rows // 4
    offset = (0, piece, piece + small)
    length = (piece, small, small)
    scale = 1.0 / math.sqrt(HEAD)
    peer = [m, m + 1 - 2 * (m % 2), (m + 2) % groups, groups - 1 - m]
    top = z == tiers - 1
    ends = (z == 0) | top
    final = jnp.where(top, tiers - 2, tiers - 1)

    def columns(member):
        return pl.ds(pl.multiple_of(member * cols, HEAD), cols)

    own = pltpu.make_async_copy(x_hbm, hid.at[z], own_sem)
    own.start()

    def weights(j):
        return pltpu.make_async_copy(w_ref.at[:, :, columns(peer[j])], wbuf.at[j], w_sem.at[j])

    for j in (3, 1, 2, 0):
        weights(j).start()
    segments = pltpu.make_async_copy(seg_hbm, seg_ref, small_sem.at[0])
    segments.start()
    flags = pltpu.make_async_copy(flag_hbm, flag_ref, small_sem.at[1])
    flags.start()

    barrier = pltpu.get_barrier_semaphore()

    @pl.when(z > 0)
    def _():
        pl.semaphore_signal(barrier, inc=1, device_id={"tok": z - 1}, device_id_type=MESH)

    @pl.when(z < tiers - 1)
    def _():
        pl.semaphore_signal(barrier, inc=1, device_id={"tok": z + 1}, device_id_type=MESH)

    for j in (1, 2):
        pl.semaphore_signal(barrier, inc=1, device_id={"mp": peer[j]}, device_id_type=MESH)
    pl.semaphore_signal(barrier, inc=1, device_id={"phase": 1 - p}, device_id_type=MESH)

    def upward(t, q):
        ref = hid.at[t, pl.ds(offset[q], length[q])]
        return remote(ref, ref, up_sem.at[t, q], gather_sem.at[t, q], {"tok": z + 1})

    def downward(t, q):
        ref = hid.at[t, pl.ds(offset[q], length[q])]
        return remote(ref, ref, down_sem.at[t, q], gather_sem.at[t, q], {"tok": z - 1})

    def arrive(t, q, onward):
        @pl.when(t < z)
        def _():
            upward(t, q).wait_recv()
            if onward:
                upward(t, q).start()

        @pl.when(t > z)
        def _():
            downward(t, q).wait_recv()
            if onward:
                downward(t, q).start()

    def arrive_half(n, onward):
        t, c = place(n)

        @pl.when(c == 0)
        def _():
            arrive(t, 0, onward)

        @pl.when(c == 1)
        def _():
            arrive(t, 1, onward)
            arrive(t, 2, onward)

    def place(n):
        c = n % 2
        inner = (n >= 2) & (n < 6)
        t1 = jnp.where(n < 2, 1, jnp.where(inner, 2 * c, 3))
        c1 = jnp.where(inner, (n - 2) // 2, c)
        t2 = jnp.where(n < 2, z, jnp.where((n == 2) | (n == 7), 5 - z, jnp.where(n < 5, 1, 0)))
        c2 = jnp.where((n < 3) | (n == 7), c, jnp.where(n < 5, n - 3, n - 5))
        t = jnp.where(z == 0, n // 2, jnp.where(z == 1, t1, t2))
        return t, jnp.where(z == 0, c, jnp.where(z == 1, c1, c2))

    def whole(n):
        t, c = place(n)
        return t, pl.ds(pl.multiple_of(c * piece, piece), piece), c

    def ending(q):
        return final, pl.ds(offset[q], length[q]), q

    def first(j, block):
        t, span, q = block
        return remote(
            send1.at[j - 1, t, span], recv1.at[j - 1, t, span],
            s1_send.at[j - 1, t, q], s1_recv.at[j - 1, t, q], {"mp": peer[j]},
        )

    def second(j, block):
        t, span, q = block
        return remote(
            send2.at[j - 1, t, span], recv2.at[j - 1, t, span],
            s2_send.at[j - 1, t, q], s2_recv.at[j - 1, t, q], {"mp": peer[j]},
        )

    def multiply(j, t, span):
        for k in range(3):
            at = slice(k * half, (k + 1) * half)
            later = slice(part3 + k * half, part3 + (k + 1) * half)
            got = jnp.dot(hid[t, span, :], wbuf[j, k], preferred_element_type=jnp.float32)
            if j == 0:
                acc[0, t, span, at] = got[:, :half]
                acc[1, t, span, at] = got[:, half:]
            elif j == 3:
                send1[0, t, span, later] = got[:, :half].astype(jnp.bfloat16)
                send1[1, t, span, later] = got[:, half:].astype(jnp.bfloat16)
            elif j == 1:
                send1[0, t, span, at] = got[:, :half].astype(jnp.bfloat16)
                keep[0, t, span, at] = got[:, half:]
            else:
                send1[1, t, span, at] = got[:, half:].astype(jnp.bfloat16)
                keep[1, t, span, at] = got[:, :half]

    def project(block):
        t, span, _ = block
        multiply(3, t, span)
        for j in (1, 2):
            multiply(j, t, span)
            first(j, block).start()
        multiply(0, t, span)

    def combine(block):
        t, span, _ = block
        for j in (1, 2):
            first(j, block).wait_recv()
        for j in (1, 2):
            got = recv1[2 - j, t, span, part3:].astype(jnp.float32)
            send2[j - 1, t, span, :] = (keep[j - 1, t, span, :] + got).astype(jnp.bfloat16)
            second(j, block).start()

    def finish(block):
        t, span, _ = block
        for j in (1, 2):
            second(j, block).wait_recv()
        start = pl.multiple_of(t * rows + span.start, small)
        for h in range(2):
            value = (
                acc[h, t, span, :]
                + recv1[h, t, span, :part3].astype(jnp.float32)
                + recv2[1 - h, t, span, :].astype(jnp.float32)
            ).astype(jnp.bfloat16)
            for k in range(3):
                qkv[k, pl.ds(start, span.size), h * half : (h + 1) * half] = value[
                    :, k * half : (k + 1) * half
                ]

    own.wait()
    everything = pl.ds(0, rows)
    for j in (3, 1):
        weights(j).wait()
        multiply(j, z, everything)

    pl.semaphore_wait(barrier, 3 + jnp.minimum(z, 1) + jnp.minimum(tiers - 1 - z, 1))

    for q in range(3):

        @pl.when((z < tiers - 2) | ((z == tiers - 2) & (q < 2)))
        def _():
            upward(z, q).start()

        @pl.when(z > 0)
        def _():
            downward(z, q).start()

    for n in range(2):
        first(1, (z, pl.ds(n * piece, piece), n)).start()
    weights(2).wait()
    multiply(2, z, everything)
    for n in range(2):
        first(2, (z, pl.ds(n * piece, piece), n)).start()
    weights(0).wait()
    multiply(0, z, everything)
    fresh = pl.multiple_of(final * rows + rows - small, small)
    qkv[2, pl.ds(fresh, small), :] = jnp.zeros((small, cols), jnp.bfloat16)

    combine(whole(0))

    @pl.loop(2, 7)
    def _(n):
        @pl.when(ends)
        def _():
            arrive_half(n, False)

        @pl.when(jnp.logical_not(ends))
        def _():
            @pl.when((n == 2) | (n == 4))
            def _():
                arrive_half(n, True)
                arrive_half(jnp.where((z == tiers - 2) & (n == 4), 7, n + 1), True)

            @pl.when((n == 6) | ((n == 5) & (z == tiers - 2)))
            def _():
                arrive_half(n, True)

            @pl.when((n == 6) & (z == tiers - 2))
            def _():
                upward(z, 2).start()

        project(whole(n))
        combine(whole(n - 1))
        finish(whole(n - 2))

    @pl.when(ends)
    def _():
        arrive(final, 1, False)

    @pl.when(z == 1)
    def _():
        arrive(final, 1, True)
        arrive(final, 2, True)

    project(ending(1))
    combine(whole(6))
    finish(whole(5))

    @pl.when(ends)
    def _():
        arrive(final, 2, False)

    project(ending(2))
    combine(ending(1))
    finish(whole(6))

    segments.wait()
    flags.wait()
    cut = (pl.ds(0, rows - small), pl.ds(rows - small, small))

    def attend_block(r, skip, keys):
        count = rows - skip
        base = pl.multiple_of(r * rows, rows)
        start = pl.multiple_of(base + skip, small)
        seg_rows = jnp.broadcast_to(seg_ref[:, pl.ds(base, rows)], (HEAD, rows)).T[skip:]
        seg_rows = jnp.concatenate([seg_rows] * (keys // HEAD), axis=1)
        key_pos = lax.broadcasted_iota(jnp.int32, (count, keys), 1)
        row_pos = lax.broadcasted_iota(jnp.int32, (count, keys), 0)
        allowed = (key_pos <= row_pos + start) & (seg_rows == seg_ref[:, :keys])
        kept = jnp.full((count, HEAD), flag_ref[0, r], jnp.int32) == 0
        for h in range(cols // HEAD):
            head = slice(h * HEAD, (h + 1) * HEAD)
            scores = (
                lax.dot_general(
                    qkv[0, pl.ds(start, count), head], qkv[1, :keys, head],
                    (((1,), (1,)), ((), ())), preferred_element_type=jnp.float32,
                )
                * scale
            )
            scores = jnp.where(allowed, scores, -1e30)
            peak = jnp.max(scores, axis=-1, keepdims=True)
            expo = jnp.exp(scores - peak)
            probs = (expo / jnp.sum(expo, axis=-1, keepdims=True)).astype(jnp.bfloat16)
            mixed = jnp.dot(probs, qkv[2, :keys, head], preferred_element_type=jnp.float32)
            outb[r, skip:, head] = jnp.where(kept, mixed, 0.0).astype(jnp.bfloat16)

    def exchange(r, j, q):
        return remote(
            outb.at[r, cut[q]], att_ref.at[cut[q], columns(m)],
            a_send.at[j - 1, q], a_recv.at[j - 1, q], {"mp": r},
        )

    def deliver(r, q):
        @pl.when(m != r)
        def _():
            exchange(r, (r + groups - m) % groups, q).start()

    def hand(j, member, q):
        here = (cut[q], columns(member))
        return remote(
            att_ref.at[here], hand_ref.at[here], h_send.at[j, q], h_recv.at[j, q], {"phase": 1 - p}
        )

    for r in range(2):
        attend_block(r, 0, (r + 1) * rows)
        deliver(r, 0)
        deliver(r, 1)

    @pl.when(jnp.logical_not(top))
    def _():
        attend_block(2, 0, 3 * rows)
        deliver(2, 0)
        deliver(2, 1)

    combine(ending(2))
    finish(ending(1))
    attend_block(final, 0, total)
    deliver(final, 0)
    finish(ending(2))
    attend_block(final, rows - small, total)
    deliver(final, 1)

    @pl.when(top)
    def _():
        attend_block(tiers - 1, 0, total)
        deliver(tiers - 1, 0)
        deliver(tiers - 1, 1)

    att_ref[:, columns(m)] = outb[m]
    for q in range(2):
        hand(0, m, q).start()
        for j in range(1, groups):
            member = (m + groups - j) % groups
            exchange(m, j, q).wait_recv()
            hand(j, member, q).start()

    for t in range(tiers):
        for q in range(3):

            @pl.when((z >= t) & (z < tiers - 1))
            def _():
                upward(t, q).wait_send()

            @pl.when((z <= t) & (z > 0))
            def _():
                downward(t, q).wait_send()

    @pl.loop(0, 7)
    def _(n):
        for j in (1, 2):
            first(j, whole(n)).wait_send()
            second(j, whole(n)).wait_send()

    for j in (1, 2):
        for q in (1, 2):
            first(j, ending(q)).wait_send()
            second(j, ending(q)).wait_send()

    for q in range(2):
        for j in range(1, groups):
            exchange((m + j) % groups, j, q).wait_send()
        for j in range(groups):
            hand(j, m, q).wait()


def local_fused(hidden, w_qkv, segment_ids, exit_flags):
    rows = hidden[0]
    weights = jnp.transpose(w_qkv[0], (1, 0, 2))
    tiers = lax.axis_size("tok")
    groups = lax.axis_size("mp")
    count, width = rows.shape
    head_cols = weights.shape[2]
    cols = head_cols // groups
    total = count * tiers
    quarter = total // groups
    half = cols // 2
    out = jax.ShapeDtypeStruct((quarter, head_cols), jnp.bfloat16)
    dma = pltpu.SemaphoreType.DMA
    pieces = (2, tiers, 3)
    operands = [
        pltpu.with_memory_space_constraint(a, pltpu.HBM)
        for a in (rows, weights, segment_ids, exit_flags)
    ]
    attended, handed = pl.pallas_call(
        fused_kernel,
        out_shape=(out, out),
        in_specs=[pl.BlockSpec(memory_space=pltpu.HBM)] * 4,
        out_specs=(pl.BlockSpec(memory_space=pltpu.VMEM),) * 2,
        scratch_shapes=[
            pltpu.VMEM((tiers, count, width), jnp.bfloat16),
            pltpu.VMEM((groups, 3, width, cols), jnp.bfloat16),
            pltpu.VMEM(segment_ids.shape, jnp.int32),
            pltpu.SMEM(exit_flags.shape, jnp.int32),
            pltpu.VMEM((2, tiers, count, 6 * half), jnp.bfloat16),
            pltpu.VMEM((2, tiers, count, 6 * half), jnp.bfloat16),
            pltpu.VMEM((2, tiers, count, 3 * half), jnp.bfloat16),
            pltpu.VMEM((2, tiers, count, 3 * half), jnp.bfloat16),
            pltpu.VMEM((2, tiers, count, 3 * half), jnp.float32),
            pltpu.VMEM((2, tiers, count, 3 * half), jnp.float32),
            pltpu.VMEM((3, total, cols), jnp.bfloat16),
            pltpu.VMEM((groups, quarter, cols), jnp.bfloat16),
            dma(()),
            dma((2,)),
            dma((groups,)),
            dma((tiers, 3)),
            dma((tiers, 3)),
            dma((tiers, 3)),
            dma(pieces),
            dma(pieces),
            dma(pieces),
            dma(pieces),
            dma((groups - 1, 2)),
            dma((groups - 1, 2)),
            dma((groups, 2)),
            dma((groups, 2)),
        ],
        compiler_params=pltpu.CompilerParams(
            collective_id=0, has_side_effects=True, vmem_limit_bytes=40 * 1024 * 1024
        ),
    )(*operands)
    return (attended[None], handed[None])


def shifted(block, axis, distance):
    devices = range(lax.axis_size(axis))
    route = [((i - distance) % len(devices), i) for i in devices]
    return lax.ppermute(block, axis, route)


def attend(query, keys, values, query_pos, segment, key_pos):
    heads_here = query.shape[1] // HEAD
    total = keys.shape[0]
    key_heads = keys.reshape(total, heads_here, HEAD)
    value_heads = values.reshape(total, heads_here, HEAD)
    key_segment = jnp.take(segment, key_pos)
    scale = 1.0 / math.sqrt(HEAD)
    block_rows = query.shape[0]
    scores = (
        jnp.einsum(
            "rhd,shd->hrs",
            query.reshape(block_rows, heads_here, HEAD),
            key_heads,
            preferred_element_type=jnp.float32,
        )
        * scale
    )
    own_segment = jnp.take(segment, query_pos)
    allowed = (key_pos[None, :] <= query_pos[:, None]) & (
        key_segment[None, :] == own_segment[:, None]
    )
    scores = jnp.where(allowed[None], scores, -1e30)
    peak = jnp.max(scores, axis=-1, keepdims=True)
    expo = jnp.exp(scores - peak)
    probs = (expo / jnp.sum(expo, axis=-1, keepdims=True)).astype(jnp.bfloat16)
    mixed = jnp.einsum("hrs,shd->rhd", probs, value_heads, preferred_element_type=jnp.float32)
    return mixed.reshape(block_rows, heads_here * HEAD).astype(jnp.bfloat16)


def local(hidden, w_qkv, segment_ids, exit_flags):
    rows_here = hidden[0]
    weights = w_qkv[0]
    width_here = rows_here.shape[1]
    head_cols = weights.shape[2]
    flat_weights = weights.reshape(width_here, 3 * head_cols)
    segment = segment_ids[0]
    flags = exit_flags[0]
    groups = lax.axis_size("mp")
    member = lax.axis_index("mp")
    partial_value = jnp.dot(
        lax.all_gather(rows_here, "tok", axis=0, tiled=True),
        flat_weights,
        preferred_element_type=jnp.float32,
    )
    total = partial_value.shape[0]
    quarter = total // groups
    query_part = partial_value[:, :head_cols]
    key_value_part = partial_value[:, head_cols:]
    my_pos = member * quarter + jnp.arange(quarter, dtype=jnp.int32)
    my_blocks = my_pos // BLOCK
    alive = jnp.take(flags, my_blocks) == 0
    query = lax.psum_scatter(query_part, "mp", scatter_dimension=0, tiled=True).astype(jnp.bfloat16)
    mine = lax.psum_scatter(key_value_part, "mp", scatter_dimension=0, tiled=True).astype(
        jnp.bfloat16
    )
    key_value = lax.all_gather(mine, "mp", axis=0, tiled=True)
    all_pos = jnp.arange(total, dtype=jnp.int32)
    mixed = attend(
        query, key_value[:, :head_cols], key_value[:, head_cols:], my_pos, segment, all_pos
    )
    zeros = jnp.zeros((quarter, head_cols), jnp.bfloat16)
    result = jnp.where(alive[:, None], mixed, zeros)
    handed = shifted(result, "phase", 1)
    return (result[None], handed[None])


def solution(mesh):
    in_specs = (
        P("phase", "tok", "mp"),
        P("phase", "mp", None, "tok"),
        P("phase", None),
        P("phase", None),
    )
    out_specs = (P("phase", "mp", "tok"), P("phase", "mp", "tok"))
    sizes = dict(mesh.shape)

    def step(hidden, w_qkv, segment_ids, exit_flags):
        heads_here = w_qkv.shape[3] // sizes["tok"] // HEAD
        quarter = hidden.shape[1] // sizes["mp"]
        by_head = (
            heads_here % (2 * sizes["mp"]) == 0
            and quarter == BLOCK
            and (sizes["phase"], sizes["tok"], sizes["mp"]) == (2, TIERS, GROUPS)
        )
        body = local_fused if by_head else local
        return jax.shard_map(
            body, mesh=mesh, in_specs=in_specs, out_specs=out_specs, check_vma=False
        )(hidden, w_qkv, segment_ids, exit_flags)

    return step
```

```python
import math

import jax
import jax.numpy as jnp
from jax import lax
from jax.experimental import pallas as pl
from jax.experimental.pallas import tpu as pltpu
from jax.sharding import PartitionSpec as P

HEAD = 128
BLOCK = 128
TIERS = 4
GROUPS = 4
MESH = pl.DeviceIdType.MESH


def remote(src, dst, send, recv, where):
    return pltpu.make_async_remote_copy(
        src_ref=src, dst_ref=dst, send_sem=send, recv_sem=recv, device_id=where, device_id_type=MESH
    )


def fused_kernel(
    x_hbm, w_ref, seg_hbm, flag_hbm, att_ref, hand_ref,
    hid, wbuf, seg_ref, flag_ref, a_out, a_in, a_acc, b_out, b_in, b_acc, chosen, query, kv, slots, outb,
    own_sem, small_sem, w_sem, q_sem, up_sem, down_sem, gather_sem,
    as_sem, ar_sem, bs_sem, br_sem, x_send, x_recv, h_send, h_recv,
):
    p = lax.axis_index("phase")
    z = lax.axis_index("tok")
    m = lax.axis_index("mp")
    tiers = TIERS
    groups = GROUPS
    rows = x_hbm.shape[0]
    cols = w_ref.shape[2] // groups
    total = rows * tiers
    piece = rows // 2
    small = rows // 4
    scale = 1.0 / math.sqrt(HEAD)
    peer = [m, m + 1 - 2 * (m % 2), (m + 2) % groups, groups - 1 - m]
    ends = (z == 0) | (z == tiers - 1)
    low = z < tiers // 2

    def columns(member):
        return pl.ds(pl.multiple_of(member * cols, HEAD), cols)

    own = pltpu.make_async_copy(x_hbm, hid.at[z], own_sem)
    own.start()

    def weights(j):
        return pltpu.make_async_copy(
            w_ref.at[pl.ds(1, 2), :, columns(peer[j])], wbuf.at[j, pl.ds(1, 2)], w_sem.at[j]
        )

    def query_weights(j):
        return pltpu.make_async_copy(
            w_ref.at[0, :, columns(peer[j])], wbuf.at[j, 0], q_sem.at[j]
        )

    for j in (1, 2, 3, 0):
        weights(j).start()
    segments = pltpu.make_async_copy(seg_hbm, seg_ref, small_sem.at[0])
    segments.start()
    flags = pltpu.make_async_copy(flag_hbm, flag_ref, small_sem.at[1])
    flags.start()
    for j in (3, 1, 2, 0):
        query_weights(j).start()

    barrier = pltpu.get_barrier_semaphore()

    @pl.when(z > 0)
    def _():
        pl.semaphore_signal(barrier, inc=1, device_id={"tok": z - 1}, device_id_type=MESH)

    @pl.when(z < tiers - 1)
    def _():
        pl.semaphore_signal(barrier, inc=1, device_id={"tok": z + 1}, device_id_type=MESH)

    for j in (1, 2):
        pl.semaphore_signal(barrier, inc=1, device_id={"mp": peer[j]}, device_id_type=MESH)
    pl.semaphore_signal(barrier, inc=1, device_id={"phase": 1 - p}, device_id_type=MESH)

    def shard(s):
        side = jnp.where(low, z, tiers - 1 - z)
        t = jnp.where(side == 0, s, jnp.where(s < 2, 1 - s, s))
        return jnp.where(low, t, tiers - 1 - t)

    def quad(t, q):
        return hid.at[t, pl.ds(pl.multiple_of(q * small, small), small)]

    def upward(t, q):
        ref = quad(t, q)
        return remote(ref, ref, up_sem.at[t, q], gather_sem.at[t, q], {"tok": z + 1})

    def downward(t, q):
        ref = quad(t, q)
        return remote(ref, ref, down_sem.at[t, q], gather_sem.at[t, q], {"tok": z - 1})

    def arrive(s, q):
        t = shard(s)

        @pl.when(t < z)
        def _():
            upward(t, q).wait_recv()

            @pl.when(z < tiers - 1)
            def _():
                upward(t, q).start()

        @pl.when(t > z)
        def _():
            downward(t, q).wait_recv()

            @pl.when(z > 0)
            def _():
                downward(t, q).start()

    def arrive_half(s, c):
        arrive(s, 2 * c)
        arrive(s, 2 * c + 1)

    def half(c):
        return pl.ds(pl.multiple_of(c * piece, piece), piece)

    def a_rows(s, c):
        return pl.ds(pl.multiple_of(s * rows + c * piece, piece), piece)

    def a_copy(j, s, c):
        here = a_rows(s, c)
        return remote(
            a_out.at[j - 1, here], a_in.at[j - 1, here],
            as_sem.at[j - 1, 2 * s + c], ar_sem.at[j - 1, 2 * s + c], {"mp": peer[j]},
        )

    def a_multiply(j, t, span, here):
        for k in (1, 2):
            at = slice((k - 1) * cols, k * cols)
            got = jnp.dot(hid[t, span, :], wbuf[j, k], preferred_element_type=jnp.float32)
            if j == 0:
                a_acc[here, at] = got
            else:
                a_out[j - 1, here, at] = got.astype(jnp.bfloat16)

    def a_project(s, c):
        for j in (3, 1, 2, 0):
            a_multiply(j, shard(s), half(c), a_rows(s, c))
            if j > 0:
                a_copy(j, s, c).start()

    def a_finish(s, c, pending=(1, 2, 3)):
        for j in pending:
            a_copy(j, s, c).wait_recv()
        here = a_rows(s, c)
        to = pl.ds(pl.multiple_of(shard(s) * rows + c * piece, piece), piece)
        for k in range(2):
            at = slice(k * cols, (k + 1) * cols)
            value = a_acc[here, at]
            for j in range(3):
                value = value + a_in[j, here, at].astype(jnp.float32)
            kv[k, to, :] = value.astype(jnp.bfloat16)

    def alive(s):
        return flag_ref[0, shard(s)] == 0

    def pick(slot, a, b, c):
        if slot == 0:
            return jnp.where(alive(0), a, jnp.where(alive(1), b, c))
        return jnp.where(alive(3), c, jnp.where(alive(2), b, a))

    def b_copy(j, block):
        s, start, size, i = block
        here = pl.ds((s - 2) * rows + start, size)
        return remote(
            b_out.at[j - 1, here], b_in.at[j - 1, here],
            bs_sem.at[j - 1, i], br_sem.at[j - 1, i], {"mp": peer[j]},
        )

    def b_project(block):
        s, start, size, _ = block
        here = pl.ds((s - 2) * rows + start, size)
        span = pl.ds(start, size)
        rest = [hid[shard(s - 2 + d), span, :] for d in range(3)]
        chosen[:size] = pick(s - 2, *rest)
        for j in (3, 1, 2, 0):
            for k in range(3):
                at = slice(k * cols, (k + 1) * cols)
                left = chosen[:size] if k == 0 else hid[shard(s), span, :]
                got = jnp.dot(left, wbuf[j, k], preferred_element_type=jnp.float32)
                if j == 0:
                    b_acc[here, at] = got
                else:
                    b_out[j - 1, here, at] = got.astype(jnp.bfloat16)
            if j > 0:
                b_copy(j, block).start()

    def b_finish(block):
        s, start, size, _ = block
        for j in (1, 2, 3):
            b_copy(j, block).wait_recv()
        here = pl.ds((s - 2) * rows + start, size)
        to = pl.ds(pl.multiple_of(shard(s) * rows + start, small), size)
        for k in range(3):
            at = slice(k * cols, (k + 1) * cols)
            value = b_acc[here, at]
            for j in range(3):
                value = value + b_in[j, here, at].astype(jnp.float32)
            value = value.astype(jnp.bfloat16)
            if k == 0:
                query[s - 2, pl.ds(start, size), :] = value
            else:
                kv[k - 1, to, :] = value

    own.wait()
    everything = pl.ds(0, rows)
    for j in (1, 2):
        weights(j).wait()
        a_multiply(j, z, everything, everything)

    pl.semaphore_wait(barrier, 3 + jnp.minimum(z, 1) + jnp.minimum(tiers - 1 - z, 1))

    for q in range(4):

        @pl.when(z < tiers - 1)
        def _():
            upward(z, q).start()

        @pl.when(z > 0)
        def _():
            downward(z, q).start()

    for c in range(2):
        for j in (1, 2):
            a_copy(j, 0, c).start()
    for j in (3, 0):
        weights(j).wait()
        a_multiply(j, z, everything, everything)
    fresh = pl.multiple_of(shard(3) * rows + rows - small, small)
    kv[1, pl.ds(fresh, small), :] = jnp.zeros((small, cols), jnp.bfloat16)
    segments.wait()
    flags.wait()
    for j in (3, 1, 2, 0):
        query_weights(j).wait()
    for j in (1, 2):
        a_copy(j, 0, 0).wait_recv()
    for c in range(2):
        a_copy(3, 0, c).start()

    block2 = [(2, 0, piece, 0), (2, piece, piece, 1)]
    block3 = [(3, 0, piece, 2), (3, piece, small, 3), (3, piece + small, small, 4)]

    @pl.when(ends)
    def _():
        arrive_half(1, 0)
        a_project(1, 0)
        arrive_half(1, 1)
        a_project(1, 1)
        a_finish(0, 0, (3,))
        a_finish(0, 1)
        arrive_half(2, 0)
        b_project(block2[0])
        a_finish(1, 0)

    @pl.when(jnp.logical_not(ends))
    def _():
        arrive_half(2, 0)
        arrive_half(1, 0)
        a_project(1, 0)
        b_project(block2[0])
        a_finish(0, 0, (3,))
        a_finish(0, 1)
        arrive_half(2, 1)
        arrive_half(1, 1)
        a_project(1, 1)
        a_finish(1, 0)

    @pl.when(ends)
    def _():
        arrive_half(2, 1)

    b_project(block2[1])
    b_finish(block2[0])
    arrive_half(3, 0)
    b_project(block3[0])
    a_finish(1, 1)
    arrive(3, 2)
    b_project(block3[1])
    b_finish(block2[1])
    arrive(3, 3)
    b_project(block3[2])

    blocks = [pick(i, shard(i), shard(i + 1), shard(i + 2)) for i in range(2)]

    def attend(i, skip, keys):
        count = rows - skip
        seg_rows = seg_ref[:, :rows]
        for r in range(1, tiers):
            seg_rows = jnp.where(blocks[i] == r, seg_ref[:, r * rows : (r + 1) * rows], seg_rows)
        seg_rows = jnp.broadcast_to(seg_rows, (HEAD, rows)).T[skip:]
        seg_rows = jnp.concatenate([seg_rows] * (keys // HEAD), axis=1)
        key_pos = lax.broadcasted_iota(jnp.int32, (count, keys), 1)
        row_pos = lax.broadcasted_iota(jnp.int32, (count, keys), 0)
        first = blocks[i] * rows + skip
        allowed = (key_pos <= row_pos + first) & (seg_rows == seg_ref[:, :keys])
        for h in range(cols // HEAD):
            head = slice(h * HEAD, (h + 1) * HEAD)
            scores = (
                lax.dot_general(
                    query[i, skip:, head], kv[0, :keys, head],
                    (((1,), (1,)), ((), ())), preferred_element_type=jnp.float32,
                )
                * scale
            )
            scores = jnp.where(allowed, scores, -1e30)
            peak = jnp.max(scores, axis=-1, keepdims=True)
            expo = jnp.exp(scores - peak)
            probs = (expo / jnp.sum(expo, axis=-1, keepdims=True)).astype(jnp.bfloat16)
            mixed = jnp.dot(probs, kv[1, :keys, head], preferred_element_type=jnp.float32)
            slots[i, skip:, head] = mixed.astype(jnp.bfloat16)

    cut = (pl.ds(0, rows - small), pl.ds(rows - small, small))

    def exchange(r, j, q):
        return remote(
            outb.at[r, cut[q]], att_ref.at[cut[q], columns(m)],
            x_send.at[j - 1, q], x_recv.at[j - 1, q], {"mp": r},
        )

    def deliver(q):
        for r in range(groups):
            rest = jnp.where(blocks[1] == r, slots[1, cut[q], :], jnp.zeros((cut[q].size, cols), jnp.bfloat16))
            outb[r, cut[q], :] = jnp.where(blocks[0] == r, slots[0, cut[q], :], rest)

            @pl.when(m != r)
            def _():
                exchange(r, (r + groups - m) % groups, q).start()

    def hand(j, member, q):
        here = (cut[q], columns(member))
        return remote(
            att_ref.at[here], hand_ref.at[here], h_send.at[j, q], h_recv.at[j, q], {"phase": 1 - p}
        )

    @pl.when(low)
    def _():
        attend(0, 0, total - rows)

    b_finish(block3[0])
    b_finish(block3[1])

    @pl.when(low)
    def _():
        attend(1, 0, total)
        deliver(0)

    b_finish(block3[2])

    @pl.when(low)
    def _():
        attend(1, rows - small, total)
        deliver(1)

    @pl.when(jnp.logical_not(low))
    def _():
        attend(0, 0, total)
        attend(1, 0, total)
        deliver(0)
        deliver(1)

    att_ref[:, columns(m)] = outb[m]
    for q in range(2):
        hand(0, m, q).start()
        for j in range(1, groups):
            member = (m + groups - j) % groups
            exchange(m, j, q).wait_recv()
            hand(j, member, q).start()

    @pl.loop(0, 4)
    def _(q):
        for t in range(tiers):

            @pl.when((z >= t) & (z < tiers - 1))
            def _():
                upward(t, q).wait_send()

            @pl.when((z <= t) & (z > 0))
            def _():
                downward(t, q).wait_send()

    for j in (1, 2, 3):
        for s in range(2):
            for c in range(2):
                a_copy(j, s, c).wait_send()
        for block in block2 + block3:
            b_copy(j, block).wait_send()

    for q in range(2):
        for j in range(1, groups):
            exchange((m + j) % groups, j, q).wait_send()
        for j in range(groups):
            hand(j, m, q).wait()


def local_fused(hidden, w_qkv, segment_ids, exit_flags):
    rows = hidden[0]
    weights = jnp.transpose(w_qkv[0], (1, 0, 2))
    tiers = lax.axis_size("tok")
    groups = lax.axis_size("mp")
    count, width = rows.shape
    head_cols = weights.shape[2]
    cols = head_cols // groups
    total = count * tiers
    quarter = total // groups
    out = jax.ShapeDtypeStruct((quarter, head_cols), jnp.bfloat16)
    dma = pltpu.SemaphoreType.DMA
    operands = [
        pltpu.with_memory_space_constraint(a, pltpu.HBM)
        for a in (rows, weights, segment_ids, exit_flags)
    ]
    attended, handed = pl.pallas_call(
        fused_kernel,
        out_shape=(out, out),
        in_specs=[pl.BlockSpec(memory_space=pltpu.HBM)] * 4,
        out_specs=(pl.BlockSpec(memory_space=pltpu.VMEM),) * 2,
        scratch_shapes=[
            pltpu.VMEM((tiers, count, width), jnp.bfloat16),
            pltpu.VMEM((groups, 3, width, cols), jnp.bfloat16),
            pltpu.VMEM(segment_ids.shape, jnp.int32),
            pltpu.SMEM(exit_flags.shape, jnp.int32),
            pltpu.VMEM((groups - 1, 2 * count, 2 * cols), jnp.bfloat16),
            pltpu.VMEM((groups - 1, 2 * count, 2 * cols), jnp.bfloat16),
            pltpu.VMEM((2 * count, 2 * cols), jnp.float32),
            pltpu.VMEM((groups - 1, 2 * count, 3 * cols), jnp.bfloat16),
            pltpu.VMEM((groups - 1, 2 * count, 3 * cols), jnp.bfloat16),
            pltpu.VMEM((2 * count, 3 * cols), jnp.float32),
            pltpu.VMEM((count // 2, width), jnp.bfloat16),
            pltpu.VMEM((2, count, cols), jnp.bfloat16),
            pltpu.VMEM((2, total, cols), jnp.bfloat16),
            pltpu.VMEM((2, count, cols), jnp.bfloat16),
            pltpu.VMEM((groups, quarter, cols), jnp.bfloat16),
            dma(()),
            dma((2,)),
            dma((groups,)),
            dma((groups,)),
            dma((tiers, 4)),
            dma((tiers, 4)),
            dma((tiers, 4)),
            dma((groups - 1, 4)),
            dma((groups - 1, 4)),
            dma((groups - 1, 5)),
            dma((groups - 1, 5)),
            dma((groups - 1, 2)),
            dma((groups - 1, 2)),
            dma((groups, 2)),
            dma((groups, 2)),
        ],
        compiler_params=pltpu.CompilerParams(
            collective_id=0, has_side_effects=True, vmem_limit_bytes=40 * 1024 * 1024
        ),
    )(*operands)
    return (attended[None], handed[None])


def shifted(block, axis, distance):
    devices = range(lax.axis_size(axis))
    route = [((i - distance) % len(devices), i) for i in devices]
    return lax.ppermute(block, axis, route)


def attend(query, keys, values, query_pos, segment, key_pos):
    heads_here = query.shape[1] // HEAD
    total = keys.shape[0]
    key_heads = keys.reshape(total, heads_here, HEAD)
    value_heads = values.reshape(total, heads_here, HEAD)
    key_segment = jnp.take(segment, key_pos)
    scale = 1.0 / math.sqrt(HEAD)
    block_rows = query.shape[0]
    scores = (
        jnp.einsum(
            "rhd,shd->hrs",
            query.reshape(block_rows, heads_here, HEAD),
            key_heads,
            preferred_element_type=jnp.float32,
        )
        * scale
    )
    own_segment = jnp.take(segment, query_pos)
    allowed = (key_pos[None, :] <= query_pos[:, None]) & (
        key_segment[None, :] == own_segment[:, None]
    )
    scores = jnp.where(allowed[None], scores, -1e30)
    peak = jnp.max(scores, axis=-1, keepdims=True)
    expo = jnp.exp(scores - peak)
    probs = (expo / jnp.sum(expo, axis=-1, keepdims=True)).astype(jnp.bfloat16)
    mixed = jnp.einsum("hrs,shd->rhd", probs, value_heads, preferred_element_type=jnp.float32)
    return mixed.reshape(block_rows, heads_here * HEAD).astype(jnp.bfloat16)


def local(hidden, w_qkv, segment_ids, exit_flags):
    rows_here = hidden[0]
    weights = w_qkv[0]
    width_here = rows_here.shape[1]
    head_cols = weights.shape[2]
    flat_weights = weights.reshape(width_here, 3 * head_cols)
    segment = segment_ids[0]
    flags = exit_flags[0]
    groups = lax.axis_size("mp")
    member = lax.axis_index("mp")
    partial_value = jnp.dot(
        lax.all_gather(rows_here, "tok", axis=0, tiled=True),
        flat_weights,
        preferred_element_type=jnp.float32,
    )
    total = partial_value.shape[0]
    quarter = total // groups
    query_part = partial_value[:, :head_cols]
    key_value_part = partial_value[:, head_cols:]
    my_pos = member * quarter + jnp.arange(quarter, dtype=jnp.int32)
    my_blocks = my_pos // BLOCK
    alive = jnp.take(flags, my_blocks) == 0
    query = lax.psum_scatter(query_part, "mp", scatter_dimension=0, tiled=True).astype(jnp.bfloat16)
    mine = lax.psum_scatter(key_value_part, "mp", scatter_dimension=0, tiled=True).astype(
        jnp.bfloat16
    )
    key_value = lax.all_gather(mine, "mp", axis=0, tiled=True)
    all_pos = jnp.arange(total, dtype=jnp.int32)
    mixed = attend(
        query, key_value[:, :head_cols], key_value[:, head_cols:], my_pos, segment, all_pos
    )
    zeros = jnp.zeros((quarter, head_cols), jnp.bfloat16)
    result = jnp.where(alive[:, None], mixed, zeros)
    handed = shifted(result, "phase", 1)
    return (result[None], handed[None])


def solution(mesh):
    in_specs = (
        P("phase", "tok", "mp"),
        P("phase", "mp", None, "tok"),
        P("phase", None),
        P("phase", None),
    )
    out_specs = (P("phase", "mp", "tok"), P("phase", "mp", "tok"))
    sizes = dict(mesh.shape)

    def step(hidden, w_qkv, segment_ids, exit_flags):
        heads_here = w_qkv.shape[3] // sizes["tok"] // HEAD
        quarter = hidden.shape[1] // sizes["mp"]
        by_head = (
            heads_here % sizes["mp"] == 0
            and quarter == BLOCK
            and (sizes["phase"], sizes["tok"], sizes["mp"]) == (2, TIERS, GROUPS)
        )
        body = local_fused if by_head else local
        return jax.shard_map(
            body, mesh=mesh, in_specs=in_specs, out_specs=out_specs, check_vma=False
        )(hidden, w_qkv, segment_ids, exit_flags)

    return step
```

```python
import math

import jax
import jax.numpy as jnp
from jax import lax
from jax.experimental import pallas as pl
from jax.experimental.pallas import tpu as pltpu
from jax.sharding import PartitionSpec as P

HEAD = 128
BLOCK = 128
TIERS = 4
GROUPS = 4
MESH = pl.DeviceIdType.MESH


def remote(src, dst, send, recv, where):
    return pltpu.make_async_remote_copy(
        src_ref=src, dst_ref=dst, send_sem=send, recv_sem=recv, device_id=where, device_id_type=MESH
    )


def fused_kernel(
    x_hbm, w_ref, seg_hbm, flag_hbm, out_ref,
    hid, wbuf, seg_ref, flag_ref, a_out, a_in, a_acc, b_out, b_in, b_acc, chosen, query, kv, slots, outb,
    own_sem, small_sem, w_sem, q_sem, up_sem, down_sem, gather_sem,
    as_sem, ar_sem, bs_sem, br_sem, x_send, x_recv, h_send, h_recv,
):
    p = lax.axis_index("phase")
    z = lax.axis_index("tok")
    m = lax.axis_index("mp")
    tiers = TIERS
    groups = GROUPS
    rows = x_hbm.shape[0]
    cols = w_ref.shape[2] // groups
    total = rows * tiers
    piece = rows // 2
    small = rows // 4
    scale = 1.0 / math.sqrt(HEAD)
    peer = [m, m + 1 - 2 * (m % 2), (m + 2) % groups, groups - 1 - m]
    ends = (z == 0) | (z == tiers - 1)
    inner = jnp.logical_not(ends)
    high = z >= tiers // 2
    att_ref, hand_ref = out_ref.at[0], out_ref.at[1]
    low = z < tiers // 2

    def columns(member):
        return pl.ds(pl.multiple_of(member * cols, HEAD), cols)

    own = pltpu.make_async_copy(x_hbm, hid.at[z], own_sem)
    own.start()

    def weights(j):
        return pltpu.make_async_copy(
            w_ref.at[pl.ds(1, 2), :, columns(peer[j])], wbuf.at[j, pl.ds(1, 2)], w_sem.at[j]
        )

    def query_weights(j):
        return pltpu.make_async_copy(
            w_ref.at[0, :, columns(peer[j])], wbuf.at[j, 0], q_sem.at[j]
        )

    for j in (1, 2, 3, 0):
        weights(j).start()
    segments = pltpu.make_async_copy(seg_hbm, seg_ref, small_sem.at[0])
    segments.start()
    flags = pltpu.make_async_copy(flag_hbm, flag_ref, small_sem.at[1])
    flags.start()
    for j in (3, 1, 2, 0):
        query_weights(j).start()

    barrier = pltpu.get_barrier_semaphore()

    @pl.when(z > 0)
    def _():
        pl.semaphore_signal(barrier, inc=1, device_id={"tok": z - 1}, device_id_type=MESH)

    @pl.when(z < tiers - 1)
    def _():
        pl.semaphore_signal(barrier, inc=1, device_id={"tok": z + 1}, device_id_type=MESH)

    for j in (1, 2):
        pl.semaphore_signal(barrier, inc=1, device_id={"mp": peer[j]}, device_id_type=MESH)
    pl.semaphore_signal(barrier, inc=1, device_id={"phase": 1 - p}, device_id_type=MESH)

    def shard(s):
        side = jnp.where(low, z, tiers - 1 - z)
        t = jnp.where(side == 0, s, jnp.where(s < 2, 1 - s, s))
        return jnp.where(low, t, tiers - 1 - t)

    def quad(t, q):
        return hid.at[t, pl.ds(pl.multiple_of(q * small, small), small)]

    def upward(t, q):
        ref = quad(t, q)
        return remote(ref, ref, up_sem.at[t, q], gather_sem.at[t, q], {"tok": z + 1})

    def downward(t, q):
        ref = quad(t, q)
        return remote(ref, ref, down_sem.at[t, q], gather_sem.at[t, q], {"tok": z - 1})

    def arrive(s, q):
        t = shard(s)

        @pl.when(t < z)
        def _():
            upward(t, q).wait_recv()

            @pl.when(z < tiers - 1)
            def _():
                upward(t, q).start()

        @pl.when(t > z)
        def _():
            downward(t, q).wait_recv()

            @pl.when(z > 0)
            def _():
                downward(t, q).start()

    def arrive_half(s, c):
        arrive(s, 2 * c)
        arrive(s, 2 * c + 1)

    def half(c):
        return pl.ds(pl.multiple_of(c * piece, piece), piece)

    def a_rows(s, c):
        return pl.ds(pl.multiple_of(s * rows + c * piece, piece), piece)

    def a_copy(j, s, c):
        here = a_rows(s, c)
        return remote(
            a_out.at[j - 1, here], a_in.at[j - 1, here],
            as_sem.at[j - 1, 2 * s + c], ar_sem.at[j - 1, 2 * s + c], {"mp": peer[j]},
        )

    def a_multiply(j, t, span, here):
        for k in (1, 2):
            at = slice((k - 1) * cols, k * cols)
            got = jnp.dot(hid[t, span, :], wbuf[j, k], preferred_element_type=jnp.float32)
            if j == 0:
                a_acc[here, at] = got
            else:
                a_out[j - 1, here, at] = got.astype(jnp.bfloat16)

    def a_project(s, c):
        for j in (3, 1, 2, 0):
            a_multiply(j, shard(s), half(c), a_rows(s, c))
            if j > 0:
                a_copy(j, s, c).start()

    def a_finish(s, c, pending=(1, 2, 3)):
        for j in pending:
            a_copy(j, s, c).wait_recv()
        here = a_rows(s, c)
        to = pl.ds(pl.multiple_of(shard(s) * rows + c * piece, piece), piece)
        for k in range(2):
            at = slice(k * cols, (k + 1) * cols)
            value = a_acc[here, at]
            for j in range(3):
                value = value + a_in[j, here, at].astype(jnp.float32)
            kv[k, to, :] = value.astype(jnp.bfloat16)

    def alive(s):
        return flag_ref[0, shard(s)] == 0

    def pick(slot, a, b, c):
        if slot == 0:
            return jnp.where(alive(0), a, jnp.where(alive(1), b, c))
        return jnp.where(alive(3), c, jnp.where(alive(2), b, a))

    def b_copy(j, block):
        s, start, size, i = block
        here = pl.ds((s - 2) * rows + start, size)
        return remote(
            b_out.at[j - 1, here], b_in.at[j - 1, here],
            bs_sem.at[j - 1, i], br_sem.at[j - 1, i], {"mp": peer[j]},
        )

    def b_project(block):
        s, start, size, _ = block
        here = pl.ds((s - 2) * rows + start, size)
        span = pl.ds(start, size)
        rest = [hid[shard(s - 2 + d), span, :] for d in range(3)]
        chosen[:size] = pick(s - 2, *rest)
        for j in (3, 1, 2, 0):
            for k in range(3):
                at = slice(k * cols, (k + 1) * cols)
                left = chosen[:size] if k == 0 else hid[shard(s), span, :]
                got = jnp.dot(left, wbuf[j, k], preferred_element_type=jnp.float32)
                if j == 0:
                    b_acc[here, at] = got
                else:
                    b_out[j - 1, here, at] = got.astype(jnp.bfloat16)
            if j > 0:
                b_copy(j, block).start()

    def b_finish(block):
        s, start, size, _ = block
        for j in (1, 2, 3):
            b_copy(j, block).wait_recv()
        here = pl.ds((s - 2) * rows + start, size)
        to = pl.ds(pl.multiple_of(shard(s) * rows + start, small), size)
        for k in range(3):
            at = slice(k * cols, (k + 1) * cols)
            value = b_acc[here, at]
            for j in range(3):
                value = value + b_in[j, here, at].astype(jnp.float32)
            value = value.astype(jnp.bfloat16)
            if k == 0:
                query[s - 2, pl.ds(start, size), :] = value
            else:
                kv[k - 1, to, :] = value

    own.wait()
    everything = pl.ds(0, rows)
    for j in (1, 2):
        weights(j).wait()
        a_multiply(j, z, everything, everything)

    pl.semaphore_wait(barrier, 3 + jnp.minimum(z, 1) + jnp.minimum(tiers - 1 - z, 1))

    for q in range(4):

        @pl.when(z < tiers - 1)
        def _():
            upward(z, q).start()

        @pl.when(z > 0)
        def _():
            downward(z, q).start()

    for c in range(2):
        for j in (1, 2):
            a_copy(j, 0, c).start()
    for j in (3, 0):
        weights(j).wait()
        a_multiply(j, z, everything, everything)
    fresh = pl.multiple_of(shard(3) * rows + rows - small, small)
    kv[1, pl.ds(fresh, small), :] = jnp.zeros((small, cols), jnp.bfloat16)
    segments.wait()
    flags.wait()
    for j in (3, 1, 2, 0):
        query_weights(j).wait()
    for j in (1, 2):
        a_copy(j, 0, 0).wait_recv()
    for c in range(2):
        a_copy(3, 0, c).start()

    block2 = [(2, 0, piece, 0), (2, piece, piece, 1)]
    block3 = [(3, 0, piece, 2), (3, piece, small, 3), (3, piece + small, small, 4)]

    @pl.when(ends)
    def _():
        arrive_half(1, 0)
        a_project(1, 0)
        arrive_half(1, 1)
        a_project(1, 1)
        a_finish(0, 0, (3,))
        a_finish(0, 1)
        arrive_half(2, 0)
        b_project(block2[0])
        a_finish(1, 0)

    @pl.when(inner)
    def _():
        arrive_half(2, 0)
        arrive_half(1, 0)
        a_project(1, 0)
        b_project(block2[0])
        a_finish(0, 0, (3,))
        a_finish(0, 1)
        arrive_half(2, 1)
        arrive_half(1, 1)
        a_project(1, 1)
        a_finish(1, 0)

    @pl.when(ends)
    def _():
        arrive_half(2, 1)

    b_project(block2[1])

    @pl.when(inner)
    def _():
        arrive_half(3, 0)

    b_finish(block2[0])

    @pl.when(ends)
    def _():
        arrive_half(3, 0)

    b_project(block3[0])

    @pl.when(inner)
    def _():
        arrive(3, 2)

    a_finish(1, 1)

    @pl.when(ends)
    def _():
        arrive(3, 2)

    b_project(block3[1])

    @pl.when(inner)
    def _():
        arrive(3, 3)

    b_finish(block2[1])

    @pl.when(ends)
    def _():
        arrive(3, 3)

    b_project(block3[2])

    blocks = [pick(i, shard(i), shard(i + 1), shard(i + 2)) for i in range(2)]

    def attend(i, skip, keys, heads=None):
        count = rows - skip
        seg_rows = seg_ref[:, :rows]
        for r in range(1, tiers):
            seg_rows = jnp.where(blocks[i] == r, seg_ref[:, r * rows : (r + 1) * rows], seg_rows)
        seg_rows = jnp.broadcast_to(seg_rows, (HEAD, rows)).T[skip:]
        seg_rows = jnp.concatenate([seg_rows] * (keys // HEAD), axis=1)
        key_pos = lax.broadcasted_iota(jnp.int32, (count, keys), 1)
        row_pos = lax.broadcasted_iota(jnp.int32, (count, keys), 0)
        first = blocks[i] * rows + skip
        allowed = (key_pos <= row_pos + first) & (seg_rows == seg_ref[:, :keys])
        for h in heads or range(cols // HEAD):
            head = slice(h * HEAD, (h + 1) * HEAD)
            scores = (
                lax.dot_general(
                    query[i, skip:, head], kv[0, :keys, head],
                    (((1,), (1,)), ((), ())), preferred_element_type=jnp.float32,
                )
                * scale
            )
            scores = jnp.where(allowed, scores, -1e30)
            peak = jnp.max(scores, axis=-1, keepdims=True)
            expo = jnp.exp(scores - peak)
            probs = (expo / jnp.sum(expo, axis=-1, keepdims=True)).astype(jnp.bfloat16)
            mixed = jnp.dot(probs, kv[1, :keys, head], preferred_element_type=jnp.float32)
            slots[i, skip:, head] = mixed.astype(jnp.bfloat16)

    some = [range(cols // HEAD // 2), range(cols // HEAD // 2, cols // HEAD)]
    by_rows = [(pl.ds(0, rows - small), 0, cols), (pl.ds(rows - small, small), 0, cols)]
    by_heads = [(pl.ds(0, rows), 0, cols // 2), (pl.ds(0, rows), cols // 2, cols // 2)]

    def target(member, q, cuts):
        here, left, width = cuts[q]
        return here, pl.ds(pl.multiple_of(member * cols + left, HEAD), width)

    def source(r, q, cuts):
        here, left, width = cuts[q]
        return outb.at[r, here, pl.ds(left, width)]

    def exchange(r, j, q, cuts):
        return remote(
            source(r, q, cuts), att_ref.at[target(m, q, cuts)],
            x_send.at[j - 1, q], x_recv.at[j - 1, q], {"mp": r},
        )

    def exchange_other(r, j, q, cuts):
        return remote(
            source(r, q, cuts), hand_ref.at[target(m, q, cuts)],
            h_send.at[j, q], h_recv.at[j, q], {"mp": r, "phase": 1 - p},
        )

    def hand(j, member, q, cuts):
        here = target(member, q, cuts)
        return remote(
            att_ref.at[here], hand_ref.at[here], h_send.at[j, q], h_recv.at[j, q], {"phase": 1 - p}
        )

    def deliver(q, cuts, other):
        here, left, width = cuts[q]
        span = slice(left, left + width)
        for r in range(groups):
            zeros = jnp.zeros((here.size, width), jnp.bfloat16)
            rest = jnp.where(blocks[1] == r, slots[1, here, span], zeros)
            outb[r, here, span] = jnp.where(blocks[0] == r, slots[0, here, span], rest)

            @pl.when(m != r)
            def _():
                j = (r + groups - m) % groups
                exchange(r, j, q, cuts).start()
                if other:
                    exchange_other(r, j, q, cuts).start()

    def collect(q, cuts, other):
        att_ref[target(m, q, cuts)] = source(m, q, cuts)[...]
        hand(0, m, q, cuts).start()
        for j in range(1, groups):
            member = (m + groups - j) % groups
            exchange(m, j, q, cuts).wait_recv()
            if not other:
                hand(j, member, q, cuts).start()

    def close(q, cuts):
        for j in range(1, groups):
            exchange((m + j) % groups, j, q, cuts).wait_send()
        for j in range(groups):
            hand(j, m, q, cuts).wait()

    @pl.when(low)
    def _():
        attend(0, 0, total - rows)

    b_finish(block3[0])
    b_finish(block3[1])

    @pl.when(low)
    def _():
        attend(1, 0, total)
        deliver(0, by_rows, False)

    b_finish(block3[2])

    @pl.when(low)
    def _():
        attend(1, rows - small, total)
        deliver(1, by_rows, True)
        collect(0, by_rows, False)
        collect(1, by_rows, True)

    @pl.when(high)
    def _():
        for q in range(2):
            attend(0, 0, total, some[q])
            attend(1, 0, total, some[q])
            deliver(q, by_heads, False)
        for q in range(2):
            collect(q, by_heads, False)

    @pl.loop(0, 4)
    def _(q):
        for t in range(tiers):

            @pl.when((z >= t) & (z < tiers - 1))
            def _():
                upward(t, q).wait_send()

            @pl.when((z <= t) & (z > 0))
            def _():
                downward(t, q).wait_send()

    for j in (1, 2, 3):
        for s in range(2):
            for c in range(2):
                a_copy(j, s, c).wait_send()
        for block in block2 + block3:
            b_copy(j, block).wait_send()

    @pl.when(low)
    def _():
        for q in range(2):
            close(q, by_rows)

    @pl.when(high)
    def _():
        for q in range(2):
            close(q, by_heads)


def local_fused(hidden, w_qkv, segment_ids, exit_flags):
    rows = hidden[0]
    weights = jnp.transpose(w_qkv[0], (1, 0, 2))
    tiers = lax.axis_size("tok")
    groups = lax.axis_size("mp")
    count, width = rows.shape
    head_cols = weights.shape[2]
    cols = head_cols // groups
    total = count * tiers
    quarter = total // groups
    out = jax.ShapeDtypeStruct((2, quarter, head_cols), jnp.bfloat16)
    dma = pltpu.SemaphoreType.DMA
    operands = [
        pltpu.with_memory_space_constraint(a, pltpu.HBM)
        for a in (rows, weights, segment_ids, exit_flags)
    ]
    both = pl.pallas_call(
        fused_kernel,
        out_shape=out,
        in_specs=[pl.BlockSpec(memory_space=pltpu.HBM)] * 4,
        out_specs=pl.BlockSpec(memory_space=pltpu.VMEM),
        scratch_shapes=[
            pltpu.VMEM((tiers, count, width), jnp.bfloat16),
            pltpu.VMEM((groups, 3, width, cols), jnp.bfloat16),
            pltpu.VMEM(segment_ids.shape, jnp.int32),
            pltpu.SMEM(exit_flags.shape, jnp.int32),
            pltpu.VMEM((groups - 1, 2 * count, 2 * cols), jnp.bfloat16),
            pltpu.VMEM((groups - 1, 2 * count, 2 * cols), jnp.bfloat16),
            pltpu.VMEM((2 * count, 2 * cols), jnp.float32),
            pltpu.VMEM((groups - 1, 2 * count, 3 * cols), jnp.bfloat16),
            pltpu.VMEM((groups - 1, 2 * count, 3 * cols), jnp.bfloat16),
            pltpu.VMEM((2 * count, 3 * cols), jnp.float32),
            pltpu.VMEM((count // 2, width), jnp.bfloat16),
            pltpu.VMEM((2, count, cols), jnp.bfloat16),
            pltpu.VMEM((2, total, cols), jnp.bfloat16),
            pltpu.VMEM((2, count, cols), jnp.bfloat16),
            pltpu.VMEM((groups, quarter, cols), jnp.bfloat16),
            dma(()),
            dma((2,)),
            dma((groups,)),
            dma((groups,)),
            dma((tiers, 4)),
            dma((tiers, 4)),
            dma((tiers, 4)),
            dma((groups - 1, 4)),
            dma((groups - 1, 4)),
            dma((groups - 1, 5)),
            dma((groups - 1, 5)),
            dma((groups - 1, 2)),
            dma((groups - 1, 2)),
            dma((groups, 2)),
            dma((groups, 2)),
        ],
        compiler_params=pltpu.CompilerParams(
            collective_id=0, has_side_effects=True, vmem_limit_bytes=40 * 1024 * 1024
        ),
    )(*operands)
    return (both[0:1], both[1:2])


def shifted(block, axis, distance):
    devices = range(lax.axis_size(axis))
    route = [((i - distance) % len(devices), i) for i in devices]
    return lax.ppermute(block, axis, route)


def attend(query, keys, values, query_pos, segment, key_pos):
    heads_here = query.shape[1] // HEAD
    total = keys.shape[0]
    key_heads = keys.reshape(total, heads_here, HEAD)
    value_heads = values.reshape(total, heads_here, HEAD)
    key_segment = jnp.take(segment, key_pos)
    scale = 1.0 / math.sqrt(HEAD)
    block_rows = query.shape[0]
    scores = (
        jnp.einsum(
            "rhd,shd->hrs",
            query.reshape(block_rows, heads_here, HEAD),
            key_heads,
            preferred_element_type=jnp.float32,
        )
        * scale
    )
    own_segment = jnp.take(segment, query_pos)
    allowed = (key_pos[None, :] <= query_pos[:, None]) & (
        key_segment[None, :] == own_segment[:, None]
    )
    scores = jnp.where(allowed[None], scores, -1e30)
    peak = jnp.max(scores, axis=-1, keepdims=True)
    expo = jnp.exp(scores - peak)
    probs = (expo / jnp.sum(expo, axis=-1, keepdims=True)).astype(jnp.bfloat16)
    mixed = jnp.einsum("hrs,shd->rhd", probs, value_heads, preferred_element_type=jnp.float32)
    return mixed.reshape(block_rows, heads_here * HEAD).astype(jnp.bfloat16)


def local(hidden, w_qkv, segment_ids, exit_flags):
    rows_here = hidden[0]
    weights = w_qkv[0]
    width_here = rows_here.shape[1]
    head_cols = weights.shape[2]
    flat_weights = weights.reshape(width_here, 3 * head_cols)
    segment = segment_ids[0]
    flags = exit_flags[0]
    groups = lax.axis_size("mp")
    member = lax.axis_index("mp")
    partial_value = jnp.dot(
        lax.all_gather(rows_here, "tok", axis=0, tiled=True),
        flat_weights,
        preferred_element_type=jnp.float32,
    )
    total = partial_value.shape[0]
    quarter = total // groups
    query_part = partial_value[:, :head_cols]
    key_value_part = partial_value[:, head_cols:]
    my_pos = member * quarter + jnp.arange(quarter, dtype=jnp.int32)
    my_blocks = my_pos // BLOCK
    alive = jnp.take(flags, my_blocks) == 0
    query = lax.psum_scatter(query_part, "mp", scatter_dimension=0, tiled=True).astype(jnp.bfloat16)
    mine = lax.psum_scatter(key_value_part, "mp", scatter_dimension=0, tiled=True).astype(
        jnp.bfloat16
    )
    key_value = lax.all_gather(mine, "mp", axis=0, tiled=True)
    all_pos = jnp.arange(total, dtype=jnp.int32)
    mixed = attend(
        query, key_value[:, :head_cols], key_value[:, head_cols:], my_pos, segment, all_pos
    )
    zeros = jnp.zeros((quarter, head_cols), jnp.bfloat16)
    result = jnp.where(alive[:, None], mixed, zeros)
    handed = shifted(result, "phase", 1)
    return (result[None], handed[None])


def solution(mesh):
    in_specs = (
        P("phase", "tok", "mp"),
        P("phase", "mp", None, "tok"),
        P("phase", None),
        P("phase", None),
    )
    out_specs = (P("phase", "mp", "tok"), P("phase", "mp", "tok"))
    sizes = dict(mesh.shape)

    def step(hidden, w_qkv, segment_ids, exit_flags):
        heads_here = w_qkv.shape[3] // sizes["tok"] // HEAD
        quarter = hidden.shape[1] // sizes["mp"]
        by_head = (
            heads_here % (2 * sizes["mp"]) == 0
            and quarter == BLOCK
            and (sizes["phase"], sizes["tok"], sizes["mp"]) == (2, TIERS, GROUPS)
        )
        body = local_fused if by_head else local
        return jax.shard_map(
            body, mesh=mesh, in_specs=in_specs, out_specs=out_specs, check_vma=False
        )(hidden, w_qkv, segment_ids, exit_flags)

    return step
```

```python
import math

import jax
import jax.numpy as jnp
from jax import lax
from jax.experimental import pallas as pl
from jax.experimental.pallas import tpu as pltpu
from jax.sharding import PartitionSpec as P

HEAD = 128
BLOCK = 128
TIERS = 4
GROUPS = 4
MESH = pl.DeviceIdType.MESH


def remote(src, dst, send, recv, where):
    return pltpu.make_async_remote_copy(
        src_ref=src, dst_ref=dst, send_sem=send, recv_sem=recv, device_id=where, device_id_type=MESH
    )


def fused_kernel(
    x_hbm, w_ref, seg_hbm, flag_hbm, out_ref,
    hid, wbuf, seg_ref, flag_ref, a_out, a_in, a_acc, b_out, b_in, b_acc, chosen, current, query, kv, slots, outb,
    own_sem, small_sem, w_sem, q_sem, up_sem, down_sem, gather_sem,
    as_sem, ar_sem, bs_sem, br_sem, x_send, x_recv, h_send, h_recv,
):
    p = lax.axis_index("phase")
    z = lax.axis_index("tok")
    m = lax.axis_index("mp")
    tiers = TIERS
    groups = GROUPS
    rows = x_hbm.shape[0]
    cols = w_ref.shape[2] // groups
    total = rows * tiers
    piece = rows // 2
    small = rows // 4
    scale = 1.0 / math.sqrt(HEAD)
    peer = [m, m + 1 - 2 * (m % 2), (m + 2) % groups, groups - 1 - m]
    ends = (z == 0) | (z == tiers - 1)
    inner = jnp.logical_not(ends)
    high = z >= tiers // 2
    att_ref, hand_ref = out_ref.at[0], out_ref.at[1]
    low = z < tiers // 2

    own = pltpu.make_async_copy(x_hbm, hid.at[z], own_sem)
    own.start()

    barrier = pltpu.get_barrier_semaphore()

    @pl.when(z > 0)
    def _():
        pl.semaphore_signal(barrier, inc=1, device_id={"tok": z - 1}, device_id_type=MESH)

    @pl.when(z < tiers - 1)
    def _():
        pl.semaphore_signal(barrier, inc=1, device_id={"tok": z + 1}, device_id_type=MESH)

    for j in (1, 2):
        pl.semaphore_signal(barrier, inc=1, device_id={"mp": peer[j]}, device_id_type=MESH)
    pl.semaphore_signal(barrier, inc=1, device_id={"phase": 1 - p}, device_id_type=MESH)

    def columns(member):
        return pl.ds(pl.multiple_of(member * cols, HEAD), cols)

    def weights(j):
        return pltpu.make_async_copy(
            w_ref.at[pl.ds(1, 2), :, columns(peer[j])], wbuf.at[j, pl.ds(1, 2)], w_sem.at[j]
        )

    def query_weights(j):
        return pltpu.make_async_copy(
            w_ref.at[0, :, columns(peer[j])], wbuf.at[j, 0], q_sem.at[j]
        )

    for j in (1, 2, 3, 0):
        weights(j).start()
    segments = pltpu.make_async_copy(seg_hbm, seg_ref, small_sem.at[0])
    segments.start()
    flags = pltpu.make_async_copy(flag_hbm, flag_ref, small_sem.at[1])
    flags.start()
    for j in (3, 1, 2, 0):
        query_weights(j).start()

    def shard(s):
        side = jnp.where(low, z, tiers - 1 - z)
        t = jnp.where(side == 0, s, jnp.where(s < 2, 1 - s, s))
        return jnp.where(low, t, tiers - 1 - t)

    def quad(t, q):
        return hid.at[t, pl.ds(pl.multiple_of(q * small, small), small)]

    def upward(t, q):
        ref = quad(t, q)
        return remote(ref, ref, up_sem.at[t, q], gather_sem.at[t, q], {"tok": z + 1})

    def downward(t, q):
        ref = quad(t, q)
        return remote(ref, ref, down_sem.at[t, q], gather_sem.at[t, q], {"tok": z - 1})

    def arrive(s, q):
        t = shard(s)

        @pl.when(t < z)
        def _():
            upward(t, q).wait_recv()

            @pl.when(z < tiers - 1)
            def _():
                upward(t, q).start()

        @pl.when(t > z)
        def _():
            downward(t, q).wait_recv()

            @pl.when(z > 0)
            def _():
                downward(t, q).start()

    def arrive_half(s, c):
        arrive(s, 2 * c)
        arrive(s, 2 * c + 1)

    def half(c):
        return pl.ds(pl.multiple_of(c * piece, piece), piece)

    def a_rows(s, c):
        return pl.ds(pl.multiple_of(s * rows + c * piece, piece), piece)

    def a_copy(j, s, c):
        here = a_rows(s, c)
        return remote(
            a_out.at[j - 1, here], a_in.at[j - 1, here],
            as_sem.at[j - 1, 2 * s + c], ar_sem.at[j - 1, 2 * s + c], {"mp": peer[j]},
        )

    def a_multiply(j, left, here):
        for k in (1, 2):
            at = slice((k - 1) * cols, k * cols)
            got = jnp.dot(left[...], wbuf[j, k], preferred_element_type=jnp.float32)[: here.size]
            if j == 0:
                a_acc[here, at] = got
            else:
                a_out[j - 1, here, at] = got.astype(jnp.bfloat16)

    def a_project(s, c):
        current[:piece] = hid[shard(s), half(c), :]
        for j in (3, 1, 2, 0):
            a_multiply(j, current, a_rows(s, c))
            if j > 0:
                a_copy(j, s, c).start()

    def a_finish(s, c, pending=(1, 2, 3)):
        for j in pending:
            a_copy(j, s, c).wait_recv()
        here = a_rows(s, c)
        to = pl.ds(pl.multiple_of(shard(s) * rows + c * piece, piece), piece)
        for k in range(2):
            at = slice(k * cols, (k + 1) * cols)
            value = a_acc[here, at]
            for j in range(3):
                value = value + a_in[j, here, at].astype(jnp.float32)
            kv[k, to, :] = value.astype(jnp.bfloat16)

    def alive(s):
        return flag_ref[0, shard(s)] == 0

    def pick(slot, a, b, c):
        if slot == 0:
            return jnp.where(alive(0), a, jnp.where(alive(1), b, c))
        return jnp.where(alive(3), c, jnp.where(alive(2), b, a))

    def b_copy(j, block):
        s, start, size, i = block
        here = pl.ds((s - 2) * rows + start, size)
        return remote(
            b_out.at[j - 1, here], b_in.at[j - 1, here],
            bs_sem.at[j - 1, i], br_sem.at[j - 1, i], {"mp": peer[j]},
        )

    def b_project(block):
        s, start, size, _ = block
        here = pl.ds((s - 2) * rows + start, size)
        span = pl.ds(start, size)
        rest = [hid[shard(s - 2 + d), span, :] for d in range(3)]
        current[:size] = hid[shard(s), span, :]
        chosen[:size] = pick(s - 2, *rest)
        for j in (3, 1, 2, 0):
            for k in range(3):
                at = slice(k * cols, (k + 1) * cols)
                left = chosen[...] if k == 0 else current[...]
                got = jnp.dot(left, wbuf[j, k], preferred_element_type=jnp.float32)[:size]
                if j == 0:
                    b_acc[here, at] = got
                else:
                    b_out[j - 1, here, at] = got.astype(jnp.bfloat16)
            if j > 0:
                b_copy(j, block).start()

    def b_finish(block):
        s, start, size, _ = block
        for j in (1, 2, 3):
            b_copy(j, block).wait_recv()
        here = pl.ds((s - 2) * rows + start, size)
        to = pl.ds(pl.multiple_of(shard(s) * rows + start, small), size)
        for k in range(3):
            at = slice(k * cols, (k + 1) * cols)
            value = b_acc[here, at]
            for j in range(3):
                value = value + b_in[j, here, at].astype(jnp.float32)
            value = value.astype(jnp.bfloat16)
            if k == 0:
                query[s - 2, pl.ds(start, size), :] = value
            else:
                kv[k - 1, to, :] = value

    own.wait()
    everything = pl.ds(0, rows)
    pl.semaphore_wait(barrier, 3 + jnp.minimum(z, 1) + jnp.minimum(tiers - 1 - z, 1))

    for q in range(4):

        @pl.when(z < tiers - 1)
        def _():
            upward(z, q).start()

        @pl.when(z > 0)
        def _():
            downward(z, q).start()

    for j in (1, 2):
        weights(j).wait()
        a_multiply(j, hid.at[z], everything)
        for c in range(2):
            a_copy(j, 0, c).start()
    for j in (3, 0):
        weights(j).wait()
        a_multiply(j, hid.at[z], everything)
    fresh = pl.multiple_of(shard(3) * rows + rows - piece, piece)
    kv[1, pl.ds(fresh, piece), :] = jnp.zeros((piece, cols), jnp.bfloat16)
    chosen[...] = jnp.zeros_like(chosen)
    current[...] = jnp.zeros_like(current)
    segments.wait()
    flags.wait()
    for j in (3, 1, 2, 0):
        query_weights(j).wait()
    for j in (1, 2):
        a_copy(j, 0, 0).wait_recv()
    for c in range(2):
        a_copy(3, 0, c).start()

    block2 = [(2, 0, piece, 0), (2, piece, piece, 1)]
    block3 = [(3, 0, piece, 2), (3, piece, piece, 3)]

    @pl.when(ends)
    def _():
        arrive_half(1, 0)
        a_project(1, 0)
        arrive_half(1, 1)
        a_project(1, 1)
        a_finish(0, 0, (3,))
        a_finish(0, 1)
        arrive_half(2, 0)
        b_project(block2[0])
        a_finish(1, 0)

    @pl.when(inner)
    def _():
        arrive_half(2, 0)
        arrive_half(1, 0)
        a_project(1, 0)
        b_project(block2[0])
        a_finish(0, 0, (3,))
        a_finish(0, 1)
        arrive_half(2, 1)
        arrive_half(1, 1)
        a_project(1, 1)
        a_finish(1, 0)

    @pl.when(ends)
    def _():
        arrive_half(2, 1)

    b_project(block2[1])

    @pl.when(inner)
    def _():
        arrive_half(3, 0)

    b_finish(block2[0])

    @pl.when(ends)
    def _():
        arrive_half(3, 0)

    b_project(block3[0])

    @pl.when(inner)
    def _():
        arrive_half(3, 1)

    a_finish(1, 1)

    @pl.when(ends)
    def _():
        arrive_half(3, 1)

    b_project(block3[1])
    b_finish(block2[1])

    blocks = [pick(i, shard(i), shard(i + 1), shard(i + 2)) for i in range(2)]

    def attend(i, skip, keys, heads=None):
        count = rows - skip
        seg_rows = seg_ref[:, :rows]
        for r in range(1, tiers):
            seg_rows = jnp.where(blocks[i] == r, seg_ref[:, r * rows : (r + 1) * rows], seg_rows)
        seg_rows = jnp.broadcast_to(seg_rows, (HEAD, rows)).T[skip:]
        seg_rows = jnp.concatenate([seg_rows] * (keys // HEAD), axis=1)
        key_pos = lax.broadcasted_iota(jnp.int32, (count, keys), 1)
        row_pos = lax.broadcasted_iota(jnp.int32, (count, keys), 0)
        first = blocks[i] * rows + skip
        allowed = (key_pos <= row_pos + first) & (seg_rows == seg_ref[:, :keys])
        for h in heads or range(cols // HEAD):
            head = slice(h * HEAD, (h + 1) * HEAD)
            scores = (
                lax.dot_general(
                    query[i, skip:, head], kv[0, :keys, head],
                    (((1,), (1,)), ((), ())), preferred_element_type=jnp.float32,
                )
                * scale
            )
            scores = jnp.where(allowed, scores, -1e30)
            peak = jnp.max(scores, axis=-1, keepdims=True)
            expo = jnp.exp(scores - peak)
            probs = (expo / jnp.sum(expo, axis=-1, keepdims=True)).astype(jnp.bfloat16)
            mixed = jnp.dot(probs, kv[1, :keys, head], preferred_element_type=jnp.float32)
            slots[i, skip:, head] = mixed.astype(jnp.bfloat16)

    some = [range(cols // HEAD // 2), range(cols // HEAD // 2, cols // HEAD)]
    by_rows = [(pl.ds(0, rows - piece), 0, cols), (pl.ds(rows - piece, piece), 0, cols)]
    by_heads = [(pl.ds(0, rows), 0, cols // 2), (pl.ds(0, rows), cols // 2, cols // 2)]

    def target(member, q, cuts):
        here, left, width = cuts[q]
        return here, pl.ds(pl.multiple_of(member * cols + left, HEAD), width)

    def source(r, q, cuts):
        here, left, width = cuts[q]
        return outb.at[r, here, pl.ds(left, width)]

    def exchange(r, j, q, cuts):
        return remote(
            source(r, q, cuts), att_ref.at[target(m, q, cuts)],
            x_send.at[j - 1, q], x_recv.at[j - 1, q], {"mp": r},
        )

    def exchange_other(r, j, q, cuts):
        return remote(
            source(r, q, cuts), hand_ref.at[target(m, q, cuts)],
            h_send.at[j, q], h_recv.at[j, q], {"mp": r, "phase": 1 - p},
        )

    def hand(j, member, q, cuts):
        here = target(member, q, cuts)
        return remote(
            att_ref.at[here], hand_ref.at[here], h_send.at[j, q], h_recv.at[j, q], {"phase": 1 - p}
        )

    def deliver(q, cuts, other):
        here, left, width = cuts[q]
        span = slice(left, left + width)
        for r in range(groups):
            zeros = jnp.zeros((here.size, width), jnp.bfloat16)
            rest = jnp.where(blocks[1] == r, slots[1, here, span], zeros)
            outb[r, here, span] = jnp.where(blocks[0] == r, slots[0, here, span], rest)

            @pl.when(m != r)
            def _():
                j = (r + groups - m) % groups
                exchange(r, j, q, cuts).start()
                if other:
                    exchange_other(r, j, q, cuts).start()

    def collect(q, cuts, other):
        att_ref[target(m, q, cuts)] = source(m, q, cuts)[...]
        hand(0, m, q, cuts).start()
        for j in range(1, groups):
            member = (m + groups - j) % groups
            exchange(m, j, q, cuts).wait_recv()
            if not other:
                hand(j, member, q, cuts).start()

    def close(q, cuts):
        for j in range(1, groups):
            exchange((m + j) % groups, j, q, cuts).wait_send()
        for j in range(groups):
            hand(j, m, q, cuts).wait()

    @pl.when(low)
    def _():
        attend(0, 0, total - rows)

    b_finish(block3[0])

    @pl.when(low)
    def _():
        attend(1, 0, total)
        deliver(0, by_rows, False)

    b_finish(block3[1])

    @pl.when(low)
    def _():
        attend(1, rows - piece, total)
        deliver(1, by_rows, True)
        collect(0, by_rows, False)
        collect(1, by_rows, True)

    @pl.when(high)
    def _():
        for q in range(2):
            attend(0, 0, total, some[q])
            attend(1, 0, total, some[q])
            deliver(q, by_heads, False)
        for q in range(2):
            collect(q, by_heads, False)

    @pl.loop(0, 4)
    def _(q):
        for t in range(tiers):

            @pl.when((z >= t) & (z < tiers - 1))
            def _():
                upward(t, q).wait_send()

            @pl.when((z <= t) & (z > 0))
            def _():
                downward(t, q).wait_send()

    for j in (1, 2, 3):
        for s in range(2):
            for c in range(2):
                a_copy(j, s, c).wait_send()
        for block in block2 + block3:
            b_copy(j, block).wait_send()

    @pl.when(low)
    def _():
        for q in range(2):
            close(q, by_rows)

    @pl.when(high)
    def _():
        for q in range(2):
            close(q, by_heads)


def local_fused(hidden, w_qkv, segment_ids, exit_flags):
    rows = hidden[0]
    weights = jnp.transpose(w_qkv[0], (1, 0, 2))
    tiers = lax.axis_size("tok")
    groups = lax.axis_size("mp")
    count, width = rows.shape
    head_cols = weights.shape[2]
    cols = head_cols // groups
    total = count * tiers
    quarter = total // groups
    out = jax.ShapeDtypeStruct((2, quarter, head_cols), jnp.bfloat16)
    dma = pltpu.SemaphoreType.DMA
    operands = [
        pltpu.with_memory_space_constraint(a, pltpu.HBM)
        for a in (rows, weights, segment_ids, exit_flags)
    ]
    both = pl.pallas_call(
        fused_kernel,
        out_shape=out,
        in_specs=[pl.BlockSpec(memory_space=pltpu.HBM)] * 4,
        out_specs=pl.BlockSpec(memory_space=pltpu.VMEM),
        scratch_shapes=[
            pltpu.VMEM((tiers, count, width), jnp.bfloat16),
            pltpu.VMEM((groups, 3, width, cols), jnp.bfloat16),
            pltpu.VMEM(segment_ids.shape, jnp.int32),
            pltpu.SMEM(exit_flags.shape, jnp.int32),
            pltpu.VMEM((groups - 1, 2 * count, 2 * cols), jnp.bfloat16),
            pltpu.VMEM((groups - 1, 2 * count, 2 * cols), jnp.bfloat16),
            pltpu.VMEM((2 * count, 2 * cols), jnp.float32),
            pltpu.VMEM((groups - 1, 2 * count, 3 * cols), jnp.bfloat16),
            pltpu.VMEM((groups - 1, 2 * count, 3 * cols), jnp.bfloat16),
            pltpu.VMEM((2 * count, 3 * cols), jnp.float32),
            pltpu.VMEM((count, width), jnp.bfloat16),
            pltpu.VMEM((count, width), jnp.bfloat16),
            pltpu.VMEM((2, count, cols), jnp.bfloat16),
            pltpu.VMEM((2, total, cols), jnp.bfloat16),
            pltpu.VMEM((2, count, cols), jnp.bfloat16),
            pltpu.VMEM((groups, quarter, cols), jnp.bfloat16),
            dma(()),
            dma((2,)),
            dma((groups,)),
            dma((groups,)),
            dma((tiers, 4)),
            dma((tiers, 4)),
            dma((tiers, 4)),
            dma((groups - 1, 4)),
            dma((groups - 1, 4)),
            dma((groups - 1, 4)),
            dma((groups - 1, 4)),
            dma((groups - 1, 2)),
            dma((groups - 1, 2)),
            dma((groups, 2)),
            dma((groups, 2)),
        ],
        compiler_params=pltpu.CompilerParams(
            collective_id=0, has_side_effects=True, vmem_limit_bytes=40 * 1024 * 1024
        ),
    )(*operands)
    return (both[0:1], both[1:2])


def shifted(block, axis, distance):
    devices = range(lax.axis_size(axis))
    route = [((i - distance) % len(devices), i) for i in devices]
    return lax.ppermute(block, axis, route)


def attend(query, keys, values, query_pos, segment, key_pos):
    heads_here = query.shape[1] // HEAD
    total = keys.shape[0]
    key_heads = keys.reshape(total, heads_here, HEAD)
    value_heads = values.reshape(total, heads_here, HEAD)
    key_segment = jnp.take(segment, key_pos)
    scale = 1.0 / math.sqrt(HEAD)
    block_rows = query.shape[0]
    scores = (
        jnp.einsum(
            "rhd,shd->hrs",
            query.reshape(block_rows, heads_here, HEAD),
            key_heads,
            preferred_element_type=jnp.float32,
        )
        * scale
    )
    own_segment = jnp.take(segment, query_pos)
    allowed = (key_pos[None, :] <= query_pos[:, None]) & (
        key_segment[None, :] == own_segment[:, None]
    )
    scores = jnp.where(allowed[None], scores, -1e30)
    peak = jnp.max(scores, axis=-1, keepdims=True)
    expo = jnp.exp(scores - peak)
    probs = (expo / jnp.sum(expo, axis=-1, keepdims=True)).astype(jnp.bfloat16)
    mixed = jnp.einsum("hrs,shd->rhd", probs, value_heads, preferred_element_type=jnp.float32)
    return mixed.reshape(block_rows, heads_here * HEAD).astype(jnp.bfloat16)


def local(hidden, w_qkv, segment_ids, exit_flags):
    rows_here = hidden[0]
    weights = w_qkv[0]
    width_here = rows_here.shape[1]
    head_cols = weights.shape[2]
    flat_weights = weights.reshape(width_here, 3 * head_cols)
    segment = segment_ids[0]
    flags = exit_flags[0]
    groups = lax.axis_size("mp")
    member = lax.axis_index("mp")
    partial_value = jnp.dot(
        lax.all_gather(rows_here, "tok", axis=0, tiled=True),
        flat_weights,
        preferred_element_type=jnp.float32,
    )
    total = partial_value.shape[0]
    quarter = total // groups
    query_part = partial_value[:, :head_cols]
    key_value_part = partial_value[:, head_cols:]
    my_pos = member * quarter + jnp.arange(quarter, dtype=jnp.int32)
    my_blocks = my_pos // BLOCK
    alive = jnp.take(flags, my_blocks) == 0
    query = lax.psum_scatter(query_part, "mp", scatter_dimension=0, tiled=True).astype(jnp.bfloat16)
    mine = lax.psum_scatter(key_value_part, "mp", scatter_dimension=0, tiled=True).astype(
        jnp.bfloat16
    )
    key_value = lax.all_gather(mine, "mp", axis=0, tiled=True)
    all_pos = jnp.arange(total, dtype=jnp.int32)
    mixed = attend(
        query, key_value[:, :head_cols], key_value[:, head_cols:], my_pos, segment, all_pos
    )
    zeros = jnp.zeros((quarter, head_cols), jnp.bfloat16)
    result = jnp.where(alive[:, None], mixed, zeros)
    handed = shifted(result, "phase", 1)
    return (result[None], handed[None])


def solution(mesh):
    in_specs = (
        P("phase", "tok", "mp"),
        P("phase", "mp", None, "tok"),
        P("phase", None),
        P("phase", None),
    )
    out_specs = (P("phase", "mp", "tok"), P("phase", "mp", "tok"))
    sizes = dict(mesh.shape)

    def step(hidden, w_qkv, segment_ids, exit_flags):
        heads_here = w_qkv.shape[3] // sizes["tok"] // HEAD
        quarter = hidden.shape[1] // sizes["mp"]
        by_head = (
            heads_here % (2 * sizes["mp"]) == 0
            and quarter == BLOCK
            and (sizes["phase"], sizes["tok"], sizes["mp"]) == (2, TIERS, GROUPS)
        )
        body = local_fused if by_head else local
        return jax.shard_map(
            body, mesh=mesh, in_specs=in_specs, out_specs=out_specs, check_vma=False
        )(hidden, w_qkv, segment_ids, exit_flags)

    return step
```

```python
import math

import jax
import jax.numpy as jnp
from jax import lax
from jax.experimental import pallas as pl
from jax.experimental.pallas import tpu as pltpu
from jax.sharding import PartitionSpec as P

HEAD = 128
BLOCK = 128
TIERS = 4
GROUPS = 4
MESH = pl.DeviceIdType.MESH


def remote(src, dst, send, recv, where):
    return pltpu.make_async_remote_copy(
        src_ref=src, dst_ref=dst, send_sem=send, recv_sem=recv, device_id=where, device_id_type=MESH
    )


def fused_kernel(
    x_hbm, w_ref, seg_hbm, flag_hbm, out_ref,
    hid, wbuf, seg_ref, flag_ref, a_out, a_in, a_acc, b_out, b_in, b_acc, chosen, current, query, kv, slots, outb,
    own_sem, small_sem, w_sem, q_sem, up_sem, down_sem, gather_sem,
    as_sem, ar_sem, bs_sem, br_sem, x_send, x_recv, h_send, h_recv,
):
    p = lax.axis_index("phase")
    z = lax.axis_index("tok")
    m = lax.axis_index("mp")
    tiers = TIERS
    groups = GROUPS
    rows = x_hbm.shape[0]
    cols = w_ref.shape[2] // groups
    total = rows * tiers
    piece = rows // 2
    small = rows // 4
    scale = 1.0 / math.sqrt(HEAD)
    peer = [m, m + 1 - 2 * (m % 2), (m + 2) % groups, groups - 1 - m]
    ends = (z == 0) | (z == tiers - 1)
    inner = jnp.logical_not(ends)
    high = z >= tiers // 2
    att_ref, hand_ref = out_ref.at[0], out_ref.at[1]
    low = z < tiers // 2

    own = pltpu.make_async_copy(x_hbm, hid.at[z], own_sem)
    own.start()

    barrier = pltpu.get_barrier_semaphore()

    @pl.when(z > 0)
    def _():
        pl.semaphore_signal(barrier, inc=1, device_id={"tok": z - 1}, device_id_type=MESH)

    @pl.when(z < tiers - 1)
    def _():
        pl.semaphore_signal(barrier, inc=1, device_id={"tok": z + 1}, device_id_type=MESH)

    for j in (1, 2):
        pl.semaphore_signal(barrier, inc=1, device_id={"mp": peer[j]}, device_id_type=MESH)
    pl.semaphore_signal(barrier, inc=1, device_id={"phase": 1 - p}, device_id_type=MESH)

    def columns(member):
        return pl.ds(pl.multiple_of(member * cols, HEAD), cols)

    def weights(j):
        return pltpu.make_async_copy(
            w_ref.at[pl.ds(1, 2), :, columns(peer[j])], wbuf.at[j, pl.ds(1, 2)], w_sem.at[j]
        )

    def query_weights(j):
        return pltpu.make_async_copy(
            w_ref.at[0, :, columns(peer[j])], wbuf.at[j, 0], q_sem.at[j]
        )

    for j in (1, 2, 3, 0):
        weights(j).start()
    segments = pltpu.make_async_copy(seg_hbm, seg_ref, small_sem.at[0])
    flags = pltpu.make_async_copy(flag_hbm, flag_ref, small_sem.at[1])

    def shard(s):
        side = jnp.where(low, z, tiers - 1 - z)
        t = jnp.where(side == 0, s, jnp.where(s < 2, 1 - s, s))
        return jnp.where(low, t, tiers - 1 - t)

    def quad(t, q):
        return hid.at[t, pl.ds(pl.multiple_of(q * small, small), small)]

    def upward(t, q):
        ref = quad(t, q)
        return remote(ref, ref, up_sem.at[t, q], gather_sem.at[t, q], {"tok": z + 1})

    def downward(t, q):
        ref = quad(t, q)
        return remote(ref, ref, down_sem.at[t, q], gather_sem.at[t, q], {"tok": z - 1})

    def arrive(s, q):
        t = shard(s)

        @pl.when(t < z)
        def _():
            upward(t, q).wait_recv()

            @pl.when(z < tiers - 1)
            def _():
                upward(t, q).start()

        @pl.when(t > z)
        def _():
            downward(t, q).wait_recv()

            @pl.when(z > 0)
            def _():
                downward(t, q).start()

    def arrive_half(s, c):
        arrive(s, 2 * c)
        arrive(s, 2 * c + 1)

    def half(c):
        return pl.ds(pl.multiple_of(c * piece, piece), piece)

    def a_rows(s, c):
        return pl.ds(pl.multiple_of(s * rows + c * piece, piece), piece)

    def a_copy(j, s, c):
        here = a_rows(s, c)
        return remote(
            a_out.at[j - 1, here], a_in.at[j - 1, here],
            as_sem.at[j - 1, 2 * s + c], ar_sem.at[j - 1, 2 * s + c], {"mp": peer[j]},
        )

    def a_multiply(j, left, here):
        for k in (1, 2):
            at = slice((k - 1) * cols, k * cols)
            got = jnp.dot(left[...], wbuf[j, k], preferred_element_type=jnp.float32)[: here.size]
            if j == 0:
                a_acc[here, at] = got
            else:
                a_out[j - 1, here, at] = got.astype(jnp.bfloat16)

    def a_project(s, c):
        current[:piece] = hid[shard(s), half(c), :]
        for j in (3, 1, 2, 0):
            a_multiply(j, current, a_rows(s, c))
            if j > 0:
                a_copy(j, s, c).start()

    def a_finish(s, c, pending=(1, 2, 3)):
        for j in pending:
            a_copy(j, s, c).wait_recv()
        here = a_rows(s, c)
        to = pl.ds(pl.multiple_of(shard(s) * rows + c * piece, piece), piece)
        for k in range(2):
            at = slice(k * cols, (k + 1) * cols)
            value = a_acc[here, at]
            for j in range(3):
                value = value + a_in[j, here, at].astype(jnp.float32)
            kv[k, to, :] = value.astype(jnp.bfloat16)

    def alive(s):
        return flag_ref[0, shard(s)] == 0

    def pick(slot, a, b, c):
        if slot == 0:
            return jnp.where(alive(0), a, jnp.where(alive(1), b, c))
        return jnp.where(alive(3), c, jnp.where(alive(2), b, a))

    def b_copy(j, block):
        s, start, size, i = block
        here = pl.ds((s - 2) * rows + start, size)
        return remote(
            b_out.at[j - 1, here], b_in.at[j - 1, here],
            bs_sem.at[j - 1, i], br_sem.at[j - 1, i], {"mp": peer[j]},
        )

    def b_project(block):
        s, start, size, _ = block
        here = pl.ds((s - 2) * rows + start, size)
        span = pl.ds(start, size)
        rest = [hid[shard(s - 2 + d), span, :] for d in range(3)]
        current[:size] = hid[shard(s), span, :]
        chosen[:size] = pick(s - 2, *rest)
        for j in (3, 1, 2, 0):
            for k in range(3):
                at = slice(k * cols, (k + 1) * cols)
                left = chosen[...] if k == 0 else current[...]
                got = jnp.dot(left, wbuf[j, k], preferred_element_type=jnp.float32)[:size]
                if j == 0:
                    b_acc[here, at] = got
                else:
                    b_out[j - 1, here, at] = got.astype(jnp.bfloat16)
            if j > 0:
                b_copy(j, block).start()

    def b_finish(block):
        s, start, size, _ = block
        for j in (1, 2, 3):
            b_copy(j, block).wait_recv()
        here = pl.ds((s - 2) * rows + start, size)
        to = pl.ds(pl.multiple_of(shard(s) * rows + start, small), size)
        for k in range(3):
            at = slice(k * cols, (k + 1) * cols)
            value = b_acc[here, at]
            for j in range(3):
                value = value + b_in[j, here, at].astype(jnp.float32)
            value = value.astype(jnp.bfloat16)
            if k == 0:
                query[s - 2, pl.ds(start, size), :] = value
            else:
                kv[k - 1, to, :] = value

    own.wait()
    everything = pl.ds(0, rows)
    pl.semaphore_wait(barrier, 3 + jnp.minimum(z, 1) + jnp.minimum(tiers - 1 - z, 1))

    for q in range(4):

        @pl.when(z < tiers - 1)
        def _():
            upward(z, q).start()

        @pl.when(z > 0)
        def _():
            downward(z, q).start()

    for j in (3, 1, 2, 0):
        query_weights(j).start()
    segments.start()
    flags.start()
    for j in (1, 2):
        weights(j).wait()
        a_multiply(j, hid.at[z], everything)
        for c in range(2):
            a_copy(j, 0, c).start()
    for j in (3, 0):
        weights(j).wait()
        a_multiply(j, hid.at[z], everything)
    fresh = pl.multiple_of(shard(3) * rows + rows - piece, piece)
    kv[1, pl.ds(fresh, piece), :] = jnp.zeros((piece, cols), jnp.bfloat16)
    chosen[...] = jnp.zeros_like(chosen)
    current[...] = jnp.zeros_like(current)
    segments.wait()
    flags.wait()
    for j in (3, 1, 2, 0):
        query_weights(j).wait()
    for j in (1, 2):
        a_copy(j, 0, 0).wait_recv()
    for c in range(2):
        a_copy(3, 0, c).start()

    block2 = [(2, 0, piece, 0), (2, piece, piece, 1)]
    block3 = [(3, 0, piece, 2), (3, piece, piece, 3)]

    @pl.when(ends)
    def _():
        arrive_half(1, 0)
        a_project(1, 0)
        arrive_half(1, 1)
        a_project(1, 1)
        a_finish(0, 0, (3,))
        a_finish(0, 1)
        arrive_half(2, 0)
        b_project(block2[0])
        a_finish(1, 0)

    @pl.when(inner)
    def _():
        arrive_half(2, 0)
        arrive_half(1, 0)
        a_project(1, 0)
        b_project(block2[0])
        a_finish(0, 0, (3,))
        a_finish(0, 1)
        arrive_half(2, 1)
        arrive_half(1, 1)
        a_project(1, 1)
        a_finish(1, 0)

    @pl.when(ends)
    def _():
        arrive_half(2, 1)

    b_project(block2[1])

    @pl.when(inner)
    def _():
        arrive_half(3, 0)

    b_finish(block2[0])

    @pl.when(ends)
    def _():
        arrive_half(3, 0)

    b_project(block3[0])

    @pl.when(inner)
    def _():
        arrive_half(3, 1)

    a_finish(1, 1)

    @pl.when(ends)
    def _():
        arrive_half(3, 1)

    b_project(block3[1])
    b_finish(block2[1])

    blocks = [pick(i, shard(i), shard(i + 1), shard(i + 2)) for i in range(2)]

    def attend(i, skip, keys, heads=None):
        count = rows - skip
        seg_rows = seg_ref[:, :rows]
        for r in range(1, tiers):
            seg_rows = jnp.where(blocks[i] == r, seg_ref[:, r * rows : (r + 1) * rows], seg_rows)
        seg_rows = jnp.broadcast_to(seg_rows, (HEAD, rows)).T[skip:]
        seg_rows = jnp.concatenate([seg_rows] * (keys // HEAD), axis=1)
        key_pos = lax.broadcasted_iota(jnp.int32, (count, keys), 1)
        row_pos = lax.broadcasted_iota(jnp.int32, (count, keys), 0)
        first = blocks[i] * rows + skip
        allowed = (key_pos <= row_pos + first) & (seg_rows == seg_ref[:, :keys])
        for h in heads or range(cols // HEAD):
            head = slice(h * HEAD, (h + 1) * HEAD)
            scores = (
                lax.dot_general(
                    query[i, skip:, head], kv[0, :keys, head],
                    (((1,), (1,)), ((), ())), preferred_element_type=jnp.float32,
                )
                * scale
            )
            scores = jnp.where(allowed, scores, -1e30)
            peak = jnp.max(scores, axis=-1, keepdims=True)
            expo = jnp.exp(scores - peak)
            probs = (expo / jnp.sum(expo, axis=-1, keepdims=True)).astype(jnp.bfloat16)
            mixed = jnp.dot(probs, kv[1, :keys, head], preferred_element_type=jnp.float32)
            slots[i, skip:, head] = mixed.astype(jnp.bfloat16)

    some = [range(cols // HEAD // 2), range(cols // HEAD // 2, cols // HEAD)]
    by_rows = [(pl.ds(0, rows - piece), 0, cols), (pl.ds(rows - piece, piece), 0, cols)]
    by_heads = [(pl.ds(0, rows), 0, cols // 2), (pl.ds(0, rows), cols // 2, cols // 2)]

    def target(member, q, cuts):
        here, left, width = cuts[q]
        return here, pl.ds(pl.multiple_of(member * cols + left, HEAD), width)

    def source(r, q, cuts):
        here, left, width = cuts[q]
        return outb.at[r, here, pl.ds(left, width)]

    def exchange(r, j, q, cuts):
        return remote(
            source(r, q, cuts), att_ref.at[target(m, q, cuts)],
            x_send.at[j - 1, q], x_recv.at[j - 1, q], {"mp": r},
        )

    def exchange_other(r, j, q, cuts):
        return remote(
            source(r, q, cuts), hand_ref.at[target(m, q, cuts)],
            h_send.at[j, q], h_recv.at[j, q], {"mp": r, "phase": 1 - p},
        )

    def hand(j, member, q, cuts):
        here = target(member, q, cuts)
        return remote(
            att_ref.at[here], hand_ref.at[here], h_send.at[j, q], h_recv.at[j, q], {"phase": 1 - p}
        )

    def deliver(q, cuts, other):
        here, left, width = cuts[q]
        span = slice(left, left + width)
        for r in range(groups):
            zeros = jnp.zeros((here.size, width), jnp.bfloat16)
            rest = jnp.where(blocks[1] == r, slots[1, here, span], zeros)
            outb[r, here, span] = jnp.where(blocks[0] == r, slots[0, here, span], rest)

            @pl.when(m != r)
            def _():
                j = (r + groups - m) % groups
                exchange(r, j, q, cuts).start()
                if other:
                    exchange_other(r, j, q, cuts).start()

    def collect(q, cuts, other):
        att_ref[target(m, q, cuts)] = source(m, q, cuts)[...]
        hand(0, m, q, cuts).start()
        for j in range(1, groups):
            member = (m + groups - j) % groups
            exchange(m, j, q, cuts).wait_recv()
            if not other:
                hand(j, member, q, cuts).start()

    def close(q, cuts):
        for j in range(1, groups):
            exchange((m + j) % groups, j, q, cuts).wait_send()
        for j in range(groups):
            hand(j, m, q, cuts).wait()

    @pl.when(low)
    def _():
        attend(0, 0, total - rows)

    b_finish(block3[0])

    @pl.when(low)
    def _():
        attend(1, 0, total)
        deliver(0, by_rows, False)

    b_finish(block3[1])

    @pl.when(low)
    def _():
        attend(1, rows - piece, total)
        deliver(1, by_rows, True)
        collect(0, by_rows, False)
        collect(1, by_rows, True)

    @pl.when(high)
    def _():
        for q in range(2):
            attend(0, 0, total, some[q])
            attend(1, 0, total, some[q])
            deliver(q, by_heads, False)
        for q in range(2):
            collect(q, by_heads, False)

    @pl.loop(0, 4)
    def _(q):
        for t in range(tiers):

            @pl.when((z >= t) & (z < tiers - 1))
            def _():
                upward(t, q).wait_send()

            @pl.when((z <= t) & (z > 0))
            def _():
                downward(t, q).wait_send()

    for j in (1, 2, 3):
        for s in range(2):
            for c in range(2):
                a_copy(j, s, c).wait_send()
        for block in block2 + block3:
            b_copy(j, block).wait_send()

    @pl.when(low)
    def _():
        for q in range(2):
            close(q, by_rows)

    @pl.when(high)
    def _():
        for q in range(2):
            close(q, by_heads)


def local_fused(hidden, w_qkv, segment_ids, exit_flags):
    rows = hidden[0]
    weights = jnp.transpose(w_qkv[0], (1, 0, 2))
    tiers = lax.axis_size("tok")
    groups = lax.axis_size("mp")
    count, width = rows.shape
    head_cols = weights.shape[2]
    cols = head_cols // groups
    total = count * tiers
    quarter = total // groups
    out = jax.ShapeDtypeStruct((2, quarter, head_cols), jnp.bfloat16)
    dma = pltpu.SemaphoreType.DMA
    operands = [
        pltpu.with_memory_space_constraint(a, pltpu.HBM)
        for a in (rows, weights, segment_ids, exit_flags)
    ]
    both = pl.pallas_call(
        fused_kernel,
        out_shape=out,
        in_specs=[pl.BlockSpec(memory_space=pltpu.HBM)] * 4,
        out_specs=pl.BlockSpec(memory_space=pltpu.VMEM),
        scratch_shapes=[
            pltpu.VMEM((tiers, count, width), jnp.bfloat16),
            pltpu.VMEM((groups, 3, width, cols), jnp.bfloat16),
            pltpu.VMEM(segment_ids.shape, jnp.int32),
            pltpu.SMEM(exit_flags.shape, jnp.int32),
            pltpu.VMEM((groups - 1, 2 * count, 2 * cols), jnp.bfloat16),
            pltpu.VMEM((groups - 1, 2 * count, 2 * cols), jnp.bfloat16),
            pltpu.VMEM((2 * count, 2 * cols), jnp.float32),
            pltpu.VMEM((groups - 1, 2 * count, 3 * cols), jnp.bfloat16),
            pltpu.VMEM((groups - 1, 2 * count, 3 * cols), jnp.bfloat16),
            pltpu.VMEM((2 * count, 3 * cols), jnp.float32),
            pltpu.VMEM((count, width), jnp.bfloat16),
            pltpu.VMEM((count, width), jnp.bfloat16),
            pltpu.VMEM((2, count, cols), jnp.bfloat16),
            pltpu.VMEM((2, total, cols), jnp.bfloat16),
            pltpu.VMEM((2, count, cols), jnp.bfloat16),
            pltpu.VMEM((groups, quarter, cols), jnp.bfloat16),
            dma(()),
            dma((2,)),
            dma((groups,)),
            dma((groups,)),
            dma((tiers, 4)),
            dma((tiers, 4)),
            dma((tiers, 4)),
            dma((groups - 1, 4)),
            dma((groups - 1, 4)),
            dma((groups - 1, 4)),
            dma((groups - 1, 4)),
            dma((groups - 1, 2)),
            dma((groups - 1, 2)),
            dma((groups, 2)),
            dma((groups, 2)),
        ],
        compiler_params=pltpu.CompilerParams(
            collective_id=0, has_side_effects=True, vmem_limit_bytes=40 * 1024 * 1024
        ),
    )(*operands)
    return (both[0:1], both[1:2])


def shifted(block, axis, distance):
    devices = range(lax.axis_size(axis))
    route = [((i - distance) % len(devices), i) for i in devices]
    return lax.ppermute(block, axis, route)


def attend(query, keys, values, query_pos, segment, key_pos):
    heads_here = query.shape[1] // HEAD
    total = keys.shape[0]
    key_heads = keys.reshape(total, heads_here, HEAD)
    value_heads = values.reshape(total, heads_here, HEAD)
    key_segment = jnp.take(segment, key_pos)
    scale = 1.0 / math.sqrt(HEAD)
    block_rows = query.shape[0]
    scores = (
        jnp.einsum(
            "rhd,shd->hrs",
            query.reshape(block_rows, heads_here, HEAD),
            key_heads,
            preferred_element_type=jnp.float32,
        )
        * scale
    )
    own_segment = jnp.take(segment, query_pos)
    allowed = (key_pos[None, :] <= query_pos[:, None]) & (
        key_segment[None, :] == own_segment[:, None]
    )
    scores = jnp.where(allowed[None], scores, -1e30)
    peak = jnp.max(scores, axis=-1, keepdims=True)
    expo = jnp.exp(scores - peak)
    probs = (expo / jnp.sum(expo, axis=-1, keepdims=True)).astype(jnp.bfloat16)
    mixed = jnp.einsum("hrs,shd->rhd", probs, value_heads, preferred_element_type=jnp.float32)
    return mixed.reshape(block_rows, heads_here * HEAD).astype(jnp.bfloat16)


def local(hidden, w_qkv, segment_ids, exit_flags):
    rows_here = hidden[0]
    weights = w_qkv[0]
    width_here = rows_here.shape[1]
    head_cols = weights.shape[2]
    flat_weights = weights.reshape(width_here, 3 * head_cols)
    segment = segment_ids[0]
    flags = exit_flags[0]
    groups = lax.axis_size("mp")
    member = lax.axis_index("mp")
    partial_value = jnp.dot(
        lax.all_gather(rows_here, "tok", axis=0, tiled=True),
        flat_weights,
        preferred_element_type=jnp.float32,
    )
    total = partial_value.shape[0]
    quarter = total // groups
    query_part = partial_value[:, :head_cols]
    key_value_part = partial_value[:, head_cols:]
    my_pos = member * quarter + jnp.arange(quarter, dtype=jnp.int32)
    my_blocks = my_pos // BLOCK
    alive = jnp.take(flags, my_blocks) == 0
    query = lax.psum_scatter(query_part, "mp", scatter_dimension=0, tiled=True).astype(jnp.bfloat16)
    mine = lax.psum_scatter(key_value_part, "mp", scatter_dimension=0, tiled=True).astype(
        jnp.bfloat16
    )
    key_value = lax.all_gather(mine, "mp", axis=0, tiled=True)
    all_pos = jnp.arange(total, dtype=jnp.int32)
    mixed = attend(
        query, key_value[:, :head_cols], key_value[:, head_cols:], my_pos, segment, all_pos
    )
    zeros = jnp.zeros((quarter, head_cols), jnp.bfloat16)
    result = jnp.where(alive[:, None], mixed, zeros)
    handed = shifted(result, "phase", 1)
    return (result[None], handed[None])


def solution(mesh):
    in_specs = (
        P("phase", "tok", "mp"),
        P("phase", "mp", None, "tok"),
        P("phase", None),
        P("phase", None),
    )
    out_specs = (P("phase", "mp", "tok"), P("phase", "mp", "tok"))
    sizes = dict(mesh.shape)

    def step(hidden, w_qkv, segment_ids, exit_flags):
        heads_here = w_qkv.shape[3] // sizes["tok"] // HEAD
        quarter = hidden.shape[1] // sizes["mp"]
        by_head = (
            heads_here % (2 * sizes["mp"]) == 0
            and quarter == BLOCK
            and (sizes["phase"], sizes["tok"], sizes["mp"]) == (2, TIERS, GROUPS)
        )
        body = local_fused if by_head else local
        return jax.shard_map(
            body, mesh=mesh, in_specs=in_specs, out_specs=out_specs, check_vma=False
        )(hidden, w_qkv, segment_ids, exit_flags)

    return step
```
